512 devices in a mesh: grp: 16 (over x, z_hi, core), dev: 32 (over y, z_lo).
Axes of the slice: x: 4, y: 8, z: 8 (z_hi: 2, z_lo: 4; z = z_hi * 4 + z_lo), core: 2. Of those that a mesh axis runs over, the one named last changes fastest.
Arguments:
- adjoint: bfloat16 [1024, 30, 192], P(('grp', 'dev')), may hold values from -6 to 6
- jacobian_tiles: bfloat16 [1024, 17, 36864], P(('grp', 'dev'))
- columns: int32 [1024, 16], P(('grp', 'dev')), may hold values from 0 to 127, as said below
- cell_rates: float32 [1024, 192], P(('grp', 'dev')), may hold values from 0.05 to 0.5
- precond: bfloat16 [1024, 36864], P(('grp', 'dev')), may hold values from -0.4375 to 0.4375
- lower_list: int32 [16, 32], replicated, may hold values from 0 to 63, as said below
- upper_list: int32 [16, 32], replicated, may hold values from 0 to 63, as said below
Outputs:
- preconditioned: bfloat16 [1024, 30, 192], P(('grp', 'dev'))
The draws below stay inside these ranges and needn't reach their ends.
Inputs may be any that keep to these rules, and one draw needn't show every extreme that they name: `columns`: rows of the first group name no value in 64 .. 95, rows of the last group no value of 96 or more. `lower_list`: the entries of a row are distinct. `upper_list`: the entries of a row are distinct.
All inputs are finite; a program needn't handle non-finite values.
Results may differ from the reference program's by a relative error of at most 0.005.
Values sent between devices are 32-bit elements; how exact they have to be, the bound alone decides.
No kernel may reach another device: no remote copies, remote signals or barrier semaphores. Data moves between devices by JAX's collectives and lax.ppermute only.
A program may use at most 64 MiB of HBM per device.

```python
import math
import jax
import jax.numpy as jnp
from jax import lax

INST = 15
ADJ = 2
DEGREE = 16
TILE = 192
ROWS = 30
GROUP_BLOCKS = 64
HALO = 32
GROUPS = 16
BLOCKS = 1024


def draw_jacobian_tiles(key, part):
    tile_shape = (BLOCKS, DEGREE + 1, TILE, TILE)
    jitter = jax.random.normal(key, tile_shape, jnp.float32)
    jitter = jitter * (0.5 / math.sqrt(TILE))
    identity = (jnp.arange(TILE)[:, None] == jnp.arange(TILE)[None, :]).astype(jnp.float32)
    self_slot = (jnp.arange(DEGREE + 1) == 0).astype(jnp.float32)
    tiles = jitter + 2.0 * self_slot[None, :, None, None] * identity[None, None]
    return tiles.reshape(BLOCKS, DEGREE + 1, TILE * TILE).astype(jnp.bfloat16)


def draw_columns(key, part):
    slot_span = GROUP_BLOCKS + 2 * HALO
    drawn = jax.random.randint(key, (BLOCKS, DEGREE), 0, slot_span)
    owner_group = (jnp.arange(BLOCKS) // GROUP_BLOCKS)[:, None]
    lower_slot = (drawn >= GROUP_BLOCKS) & (drawn < GROUP_BLOCKS + HALO)
    upper_slot = drawn >= GROUP_BLOCKS + HALO
    drawn = jnp.where((owner_group == 0) & lower_slot, drawn - GROUP_BLOCKS, drawn)
    drawn = jnp.where((owner_group == GROUPS - 1) & upper_slot, drawn - GROUP_BLOCKS - HALO, drawn)
    drawn = drawn.at[0, DEGREE - 1].set(slot_span - 1)
    drawn = drawn.at[BLOCKS - 1, DEGREE - 1].set(GROUP_BLOCKS + HALO - 1)
    drawn = drawn.at[0, 0].set(0)
    return drawn.astype(jnp.int32)


def draw_list(key, stream_tag, marked_row):
    row_keys = jax.random.split(jax.random.fold_in(key, stream_tag), GROUPS)
    shuffled = jax.vmap(lambda row_key: jax.random.permutation(row_key, GROUP_BLOCKS))(row_keys)
    chosen = shuffled[:, :HALO]
    marked = chosen[marked_row]
    marked = jnp.where(marked == GROUP_BLOCKS - 1, marked[0], marked)
    marked = marked.at[0].set(GROUP_BLOCKS - 1)
    chosen = chosen.at[marked_row].set(marked)
    return chosen.astype(jnp.int32)


def draw_lower_list(key, part):
    return draw_list(key, 11, 1)


def draw_upper_list(key, part):
    return draw_list(key, 23, GROUPS - 2)


def block_scale(own_key, shape, pieces, least, largest):
    def one(position, parts):
        steps = jax.random.uniform(jax.random.fold_in(jax.random.fold_in(own_key, 6), position), (parts,), jnp.float32, least / len(pieces), largest / len(pieces))
        return jnp.repeat(jnp.exp(steps), shape[position] // parts).reshape((-1,) + (1,) * (len(shape) - position - 1))

    factor_of = one(*pieces[0])
    for cut in pieces[1:]:
        factor_of = factor_of * one(*cut)
    return factor_of


def normal_values(own_key, shape, scale, limit, shards=(), kind=jnp.bfloat16):
    values = jax.random.normal(own_key, shape, jnp.float32) * scale
    if len(shards) > 0:
        values = block_scale(own_key, shape, shards, -0.22, 0.18) * values
    return jnp.clip(values, min=-limit, max=limit).astype(kind)


def setup_inputs(seed: int = 0) -> dict:
    splits = jax.random.split(jax.random.key(seed), 8)
    adjoint = normal_values(splits[0], (BLOCKS, ROWS, TILE), 1.0, 6.0, ((0, 512),))
    jacobian_tiles = draw_jacobian_tiles(jax.random.fold_in(splits[7], 71), 0)
    columns = draw_columns(jax.random.fold_in(splits[7], 71), 0)
    cell_rates = jnp.clip(jnp.exp(math.log(0.5) - 2.3025851 * jax.random.uniform(splits[3], (BLOCKS, TILE), jnp.float32) ** block_scale(splits[3], (BLOCKS, TILE), ((0, 512),), -0.2, 0.2)), 0.05, 0.5)
    precond = normal_values(splits[4], (BLOCKS, TILE * TILE), TILE ** -0.5, 0.4375, ((0, 512),))
    lower_list = draw_lower_list(jax.random.fold_in(splits[7], 71), 0)
    upper_list = draw_upper_list(jax.random.fold_in(splits[7], 71), 0)
    return dict(adjoint=adjoint, jacobian_tiles=jacobian_tiles, columns=columns, cell_rates=cell_rates, precond=precond, lower_list=lower_list, upper_list=upper_list)


def spectral_matrix(length):
    row_index = jnp.arange(length)[:, None]
    col_index = jnp.arange(length)[None, :]
    offset = row_index - col_index
    parity = jnp.where(offset % 2 == 0, 1.0, -1.0).astype(jnp.float32)
    phase_angle = (jnp.pi / length) * offset.astype(jnp.float32)
    sine_values = jnp.where(offset == 0, 1.0, jnp.sin(phase_angle))
    return jnp.where(offset == 0, 0.0, 0.5 * parity / sine_values).astype(jnp.float32)


def place_terms(targets, values):
    return jnp.zeros((GROUP_BLOCKS, ROWS, TILE), jnp.float32).at[targets].add(values)


def reference(adjoint, jacobian_tiles, columns, cell_rates, precond, lower_list, upper_list):
    slot_span = GROUP_BLOCKS + 2 * HALO
    local_ids = jnp.arange(GROUP_BLOCKS, dtype=jnp.int32)
    square_tiles = jacobian_tiles.reshape(BLOCKS, DEGREE + 1, TILE, TILE)
    square_precond = precond.reshape(BLOCKS, TILE, TILE)

    def one_group(group_index):
        row_start = (group_index * GROUP_BLOCKS).astype(jnp.int32)
        adjoint_part = lax.dynamic_slice_in_dim(adjoint, row_start, GROUP_BLOCKS, 0).astype(jnp.float32)
        tile_part = lax.dynamic_slice_in_dim(square_tiles, row_start, GROUP_BLOCKS, 0).astype(jnp.float32)
        column_part = lax.dynamic_slice_in_dim(columns, row_start, GROUP_BLOCKS, 0)
        products = jnp.einsum("brt,bkts->bkrs", adjoint_part, tile_part, precision=lax.Precision.HIGHEST)
        targets = jnp.concatenate([local_ids[:, None], column_part], axis=1).reshape(-1)
        return jax.ops.segment_sum(products.reshape(GROUP_BLOCKS * (DEGREE + 1), ROWS, TILE), targets, num_segments=slot_span)

    collected = lax.map(one_group, jnp.arange(GROUPS, dtype=jnp.int32))
    interior = collected[:, :GROUP_BLOCKS]
    lower_terms = collected[1:, GROUP_BLOCKS:GROUP_BLOCKS + HALO]
    upper_terms = collected[:-1, GROUP_BLOCKS + HALO:]
    from_above = jax.vmap(place_terms)(lower_list[1:], lower_terms)
    from_below = jax.vmap(place_terms)(upper_list[:-1], upper_terms)
    empty_group = jnp.zeros((1, GROUP_BLOCKS, ROWS, TILE), jnp.float32)
    interior = interior + jnp.concatenate([from_above, empty_group], 0) + jnp.concatenate([empty_group, from_below], 0)
    transposed = interior.reshape(BLOCKS, ROWS, TILE)
    spectral = spectral_matrix(INST)
    instances = adjoint.astype(jnp.float32).reshape(BLOCKS, ADJ, INST, TILE)
    spectral_part = jnp.einsum("nm,bant->bamt", spectral, instances, precision=lax.Precision.HIGHEST)
    spectral_part = cell_rates[:, None, None, :] * spectral_part
    combined = (transposed + spectral_part.reshape(BLOCKS, ROWS, TILE)).astype(jnp.bfloat16)
    result = jnp.einsum("brt,bts->brs", combined.astype(jnp.float32), square_precond.astype(jnp.float32), precision=lax.Precision.HIGHEST)
    return result.astype(jnp.bfloat16)
```

```python
import jax
import jax.numpy as jnp
from jax import lax
from jax.sharding import PartitionSpec as P

INST = 15
ADJ = 2


def passed_along(value, axis, by):
    length = lax.axis_size(axis)
    pairs = [(i, i + by) for i in range(length) if 0 <= i + by < length]
    return lax.ppermute(value, axis, pairs)


def spectral_matrix(length):
    row_index = jnp.arange(length)[:, None]
    col_index = jnp.arange(length)[None, :]
    offset = row_index - col_index
    parity = jnp.where(offset % 2 == 0, 1.0, -1.0).astype(jnp.float32)
    phase_angle = jnp.pi / length * offset.astype(jnp.float32)
    sine_values = jnp.where(offset == 0, 1.0, jnp.sin(phase_angle))
    return jnp.where(offset == 0, 0.0, 0.5 * parity / sine_values)


def shards(adjoint, jacobian_tiles, columns, cell_rates, precond, lower_list, upper_list):
    blocks, row_count, tile_width = adjoint.shape
    tile_slots = jacobian_tiles.shape[1]
    square_tiles = jacobian_tiles.reshape(blocks, tile_slots, tile_width, tile_width)
    square_precond = precond.reshape(blocks, tile_width, tile_width)
    members = lax.axis_size("dev")
    group_blocks = blocks * members
    groups = lower_list.shape[0]
    halo_slots = lower_list.shape[1]
    member = lax.axis_index("dev")
    group_id = lax.axis_index("grp")
    products = jnp.einsum(
        "brt,bkts->bkrs", adjoint, square_tiles, preferred_element_type=jnp.float32
    )
    flat_terms = products.reshape(blocks * tile_slots, row_count * tile_width)
    own_ids = member * blocks + jnp.arange(blocks, dtype=jnp.int32)
    targets = jnp.concatenate([own_ids[:, None], columns], axis=1).reshape(-1)
    slot_ids = group_blocks + jnp.arange(2 * halo_slots, dtype=jnp.int32)
    picker = (slot_ids[:, None] == targets[None, :]).astype(jnp.float32)
    halo_terms = jnp.dot(
        picker, flat_terms, precision=lax.Precision.HIGHEST, preferred_element_type=jnp.float32
    )
    upper_group = jnp.minimum(group_id + 1, groups - 1)
    lower_group = jnp.maximum(group_id - 1, 0)
    from_above = passed_along(halo_terms[:halo_slots], "grp", -1)
    from_below = passed_along(halo_terms[halo_slots:], "grp", 1)
    lower_ids = lax.dynamic_slice(lower_list, (upper_group, 0), (1, halo_slots))[0]
    upper_ids = lax.dynamic_slice(upper_list, (lower_group, 0), (1, halo_slots))[0]
    incoming = jnp.concatenate([from_above, from_below], axis=0)
    incoming_ids = jnp.concatenate([lower_ids, upper_ids])
    positions = jnp.arange(blocks * lax.axis_size("dev"), dtype=jnp.int32)
    own_rows = (positions[:, None] == targets[None, :]).astype(jnp.float32)
    halo_rows = (positions[:, None] == incoming_ids[None, :]).astype(jnp.float32)
    local_sum = jnp.dot(
        own_rows, flat_terms, precision=lax.Precision.HIGHEST, preferred_element_type=jnp.float32
    )
    dense = local_sum + jnp.dot(
        halo_rows, incoming, precision=lax.Precision.HIGHEST, preferred_element_type=jnp.float32
    )
    shared = lax.all_to_all(
        dense.reshape(members, blocks * row_count * tile_width), "dev", 0, 0, tiled=True
    )
    transposed = jnp.sum(shared, axis=0)
    spectral = spectral_matrix(INST)
    instances = adjoint.astype(jnp.float32).reshape(blocks, ADJ, INST, tile_width)
    spectral_part = jnp.einsum(
        "nm,bant->bamt", spectral, instances, precision=lax.Precision.HIGHEST
    )
    spectral_part = cell_rates[:, None, None, :] * spectral_part
    combined = (
        transposed.reshape(blocks, row_count, tile_width)
        + spectral_part.reshape(blocks, row_count, tile_width)
    ).astype(jnp.bfloat16)
    result = jnp.einsum(
        "brt,bts->brs", combined, square_precond, preferred_element_type=jnp.float32
    )
    return result.astype(jnp.bfloat16)


def solution(mesh):
    return jax.shard_map(
        shards,
        mesh=mesh,
        in_specs=(
            P(("grp", "dev"), None, None),
            P(("grp", "dev"), None, None),
            P(("grp", "dev"), None),
            P(("grp", "dev"), None),
            P(("grp", "dev"), None),
            P(),
            P(),
        ),
        out_specs=P(("grp", "dev"), None, None),
        check_vma=False,
    )
```

```python
import functools

import jax
import jax.numpy as jnp
from jax import lax
from jax.experimental import pallas as pl
from jax.experimental.pallas import tpu as pltpu
from jax.sharding import Mesh, PartitionSpec as P

INST = 15
ADJ = 2
HALO = 32
GROUP_BLOCKS = 64
AXES = ("x", "zh", "core", "y", "zl")
SIZES = (4, 2, 2, 8, 4)
PLANES = (48, 128)
OFF, INSIDE, ON = 0, 64, 128


def spectral_matrix(length):
    row_index = jnp.arange(length)[:, None]
    col_index = jnp.arange(length)[None, :]
    offset = row_index - col_index
    parity = jnp.where(offset % 2 == 0, 1.0, -1.0).astype(jnp.float32)
    phase_angle = jnp.pi / length * offset.astype(jnp.float32)
    sine_values = jnp.where(offset == 0, 1.0, jnp.sin(phase_angle))
    return jnp.where(offset == 0, 0.0, 0.5 * parity / sine_values)


def both_ways(plus, minus):
    plus, minus = lax.optimization_barrier((plus, minus))
    plus = lax.ppermute(plus, "y", [(i, (i + 1) % 8) for i in range(8)])
    minus = lax.ppermute(minus, "y", [(i, (i - 1) % 8) for i in range(8)])
    return plus, minus


def off_chip_pairs():
    pairs = []
    for g in range(16):
        t = g + 1 if g % 2 else g - 1
        if 0 <= t < 16:
            pairs += [(g * 4 + z, t * 4 + 3 - z) for z in range(4)]
    return pairs


def group_index():
    return (lax.axis_index("x") * 2 + lax.axis_index("zh")) * 2 + lax.axis_index("core")


def placed(block):
    return ((((block >> 3) - lax.axis_index("y")) & 7) << 3) + (block & 7)


def terms_kernel(columns, lower, upper, adj, tiles, dense, plus, minus, on):
    group, odd = group_index(), lax.axis_index("core")
    off_base = GROUP_BLOCKS + HALO * odd
    on_base = GROUP_BLOCKS + HALO * (1 - odd)
    for i in range(dense.shape[0]):
        dense[i] = jnp.zeros(PLANES, jnp.float32)
    for b in range(2):
        rows = adj[b]
        for k in range(17):
            term = jnp.dot(rows, tiles[k, b], preferred_element_type=jnp.float32)
            tail = jnp.concatenate([term[:16, 128:], term[16:, 128:]], axis=1)
            planes = jnp.concatenate([term[:16, :128], term[16:, :128], tail], axis=0)
            if k == 0:
                target = INSIDE + lax.axis_index("zl") * 2 + b
            else:
                c = columns[b, k - 1]
                slot = jnp.clip(c - off_base, 0, HALO - 1)
                away = jnp.where(odd == 1, upper[group, slot], lower[group, slot])
                target = jnp.where(
                    c < GROUP_BLOCKS,
                    INSIDE + placed(c),
                    jnp.where(
                        (c >= off_base) & (c < off_base + HALO),
                        OFF + placed(away),
                        ON + c - on_base,
                    ),
                )
            dense[target] += planes
    plus[...] = dense[OFF + 32 : OFF + 36]
    minus[...] = dense[OFF + 36 : OFF + 40]
    on[...] = dense[ON : ON + HALO]


def merge_kernel(lower, upper, rp, rm, got, off3, off5, inside, merged, sp, sm):
    mate, odd = group_index() ^ 1, lax.axis_index("core")
    merged[...] = inside[...]
    for h in range(HALO):
        target = placed(jnp.where(odd == 1, upper[mate, h], lower[mate, h]))
        merged[target] += got[h]
    sp[0:4] = off3[0:4] + rp[...]
    sp[4:8] = off3[4:8]
    sp[8:12] = merged[32:36]
    sm[0:4] = off5[0:4]
    sm[4:8] = off5[4:8] + rm[...]
    sm[8:12] = merged[36:40]


def third_kernel(rp, rm, off2, off6, in3, in5, sp, sm):
    sp[0:8] = off2[...] + rp[0:8]
    sp[8:12] = in3[0:4] + rp[8:12]
    sp[12:16] = in3[4:8]
    sm[0:8] = off6[...] + rm[0:8]
    sm[8:12] = in5[0:4]
    sm[12:16] = in5[4:8] + rm[8:12]


def fourth_kernel(rp, rm, off1, off7, in2, in6, sp, sm):
    sp[0:8] = off1[...] + rp[0:8]
    sp[8:16] = in2[...] + rp[8:16]
    sm[0:8] = off7[...] + rm[0:8]
    sm[8:16] = in6[...] + rm[8:16]


def fifth_kernel(rp, rm, off0, in1, in7, leaving, sp, sm):
    leaving[...] = off0[...] + rp[0:8] + rm[0:8]
    sp[...] = in1[...] + rp[8:16]
    sm[...] = in7[...] + rm[8:16]


def sum_kernel(rp, rm, crossed, in0, out):
    out[...] = in0[...] + rp[...] + rm[...] + crossed[...]


def spectral_kernel(matrix, adj, rates, out):
    for b in range(2):
        part = jnp.dot(
            matrix[...],
            adj[b].astype(jnp.float32),
            precision=lax.Precision.HIGHEST,
            preferred_element_type=jnp.float32,
        )
        out[b] = rates[b : b + 1, :] * part


def last_kernel(shared, part, precond, out):
    for b in range(2):
        total = shared[0, b] + shared[1, b] + shared[2, b] + shared[3, b]
        tail = total[32:48]
        top = jnp.concatenate([total[:16], tail[:, :64]], axis=1)
        bottom = jnp.concatenate([total[16:32], tail[:, 64:]], axis=1)
        combined = (jnp.concatenate([top, bottom], axis=0) + part[b]).astype(jnp.bfloat16)
        out[b] = jnp.dot(combined, precond[b], preferred_element_type=jnp.float32).astype(
            jnp.bfloat16
        )


def whole():
    return pl.BlockSpec(memory_space=pltpu.VMEM)


def scalars():
    return pl.BlockSpec(memory_space=pltpu.SMEM)


def blocks_of(count, start):
    return pl.BlockSpec((count,) + PLANES, lambda i: (start // count, 0, 0))


def stack(*counts):
    return [jax.ShapeDtypeStruct((n,) + PLANES, jnp.float32) for n in counts]


def combine(kernel, received, picks, counts, name):
    specs = [blocks_of(r.shape[0], 0) for r in received]
    specs += [blocks_of(n, start) for _, n, start in picks]
    return pl.pallas_call(
        kernel,
        out_shape=stack(*counts),
        grid=(1,),
        in_specs=specs,
        out_specs=[blocks_of(n, 0) for n in counts],
        compiler_params=pltpu.CompilerParams(vmem_limit_bytes=16 * 2**20),
        name=name,
    )(*received, *[a for a, _, _ in picks])


def shards(adjoint, jacobian_tiles, columns, cell_rates, precond, lower_list, upper_list):
    blocks, row_count, tile_width = adjoint.shape
    slots = jacobian_tiles.shape[1]
    tiles = jacobian_tiles.reshape(blocks, slots, tile_width, tile_width).transpose(1, 0, 2, 3)
    square_precond = precond.reshape(blocks, tile_width, tile_width)
    padded = jnp.pad(
        adjoint.reshape(blocks, ADJ, INST, tile_width), ((0, 0), (0, 0), (0, 1), (0, 0))
    ).reshape(blocks, 32, tile_width)

    dense, sp, sm, on = pl.pallas_call(
        terms_kernel,
        out_shape=stack(160, 4, 4, HALO),
        in_specs=[scalars(), scalars(), scalars(), whole(), whole()],
        out_specs=[whole()] * 4,
        compiler_params=pltpu.CompilerParams(vmem_limit_bytes=32 * 2**20),
        name="terms",
    )(columns, lower_list, upper_list, padded, tiles)
    rp, rm = both_ways(sp, sm)
    got = lax.ppermute(on, "core", [(0, 1), (1, 0)])
    inside, sp, sm = pl.pallas_call(
        merge_kernel,
        out_shape=stack(64, 12, 12),
        grid=(1,),
        in_specs=[scalars(), scalars()]
        + [blocks_of(n, 0) for n in (4, 4, HALO)]
        + [blocks_of(8, OFF + 24), blocks_of(8, OFF + 40), blocks_of(64, INSIDE)],
        out_specs=[blocks_of(n, 0) for n in (64, 12, 12)],
        compiler_params=pltpu.CompilerParams(vmem_limit_bytes=24 * 2**20),
        name="merge",
    )(lower_list, upper_list, rp, rm, got, dense, dense, dense)
    rp, rm = both_ways(sp, sm)
    sp, sm = combine(
        third_kernel,
        (rp, rm),
        ((dense, 8, OFF + 16), (dense, 8, OFF + 48), (inside, 8, 24), (inside, 8, 40)),
        (16, 16),
        "third",
    )
    rp, rm = both_ways(sp, sm)
    sp, sm = combine(
        fourth_kernel,
        (rp, rm),
        ((dense, 8, OFF + 8), (dense, 8, OFF + 56), (inside, 8, 16), (inside, 8, 48)),
        (16, 16),
        "fourth",
    )
    rp, rm = both_ways(sp, sm)
    leaving, sp, sm = combine(
        fifth_kernel,
        (rp, rm),
        ((dense, 8, OFF), (inside, 8, 8), (inside, 8, 56)),
        (8, 8, 8),
        "fifth",
    )
    crossed = lax.ppermute(leaving, ("x", "zh", "core", "zl"), off_chip_pairs())
    rp, rm = both_ways(sp, sm)
    (column_sum,) = combine(sum_kernel, (rp, rm, crossed), ((inside, 8, 0),), (8,), "total")
    shared = lax.all_to_all(column_sum.reshape(4, -1), "zl", 0, 0, tiled=True)

    half = jnp.pad(spectral_matrix(INST).T, ((0, 1), (0, 1)))
    matrix = jnp.kron(jnp.eye(ADJ, dtype=jnp.float32), half)
    part = pl.pallas_call(
        spectral_kernel,
        out_shape=jax.ShapeDtypeStruct((blocks, 32, tile_width), jnp.float32),
        in_specs=[whole()] * 3,
        out_specs=whole(),
        compiler_params=pltpu.CompilerParams(vmem_limit_bytes=8 * 2**20),
        name="spectral",
    )(matrix, padded, cell_rates)
    result = pl.pallas_call(
        last_kernel,
        out_shape=jax.ShapeDtypeStruct((blocks, 32, tile_width), jnp.bfloat16),
        in_specs=[whole()] * 3,
        out_specs=whole(),
        compiler_params=pltpu.CompilerParams(vmem_limit_bytes=8 * 2**20),
        name="last",
    )(shared.reshape(4, blocks, *PLANES), part, square_precond)
    return (
        result.reshape(blocks, ADJ, 16, tile_width)[:, :, :INST]
        .reshape(blocks, row_count, tile_width)
    )


def solution(mesh):
    split_mesh = Mesh(mesh.devices.reshape(SIZES), AXES)
    split = P(AXES)
    return jax.shard_map(
        shards,
        mesh=split_mesh,
        in_specs=(split, split, split, split, split, P(), P()),
        out_specs=split,
        check_vma=False,
    )
```

```python
import jax
import jax.numpy as jnp
from jax import lax
from jax.experimental import pallas as pl
from jax.experimental.pallas import tpu as pltpu
from jax.sharding import Mesh, PartitionSpec as P

INST = 15
ADJ = 2
HALO = 32
GROUP_BLOCKS = 64
AXES = ("x", "zh", "core", "yh", "yp", "zl")
SIZES = (4, 2, 2, 4, 2, 4)
PLANES = (48, 128)
KEEP, GIVE, OFF, ON, ROWS = 0, 32, 64, 96, 128


def spectral_matrix(length):
    row_index = jnp.arange(length)[:, None]
    col_index = jnp.arange(length)[None, :]
    offset = row_index - col_index
    parity = jnp.where(offset % 2 == 0, 1.0, -1.0).astype(jnp.float32)
    phase_angle = jnp.pi / length * offset.astype(jnp.float32)
    sine_values = jnp.where(offset == 0, 1.0, jnp.sin(phase_angle))
    return jnp.where(offset == 0, 0.0, 0.5 * parity / sine_values)


def pair_pairs():
    pairs = []
    for c in range(2):
        for y in range(8):
            mate = (((y - c) % 8) ^ 1) + c
            pairs.append((c * 8 + y, c * 8 + mate % 8))
    return pairs


def to_mate(value):
    return lax.ppermute(value, ("core", "yh", "yp"), pair_pairs())


def off_chip_pairs():
    pairs = []
    for g in range(16):
        t = g + 1 if g % 2 else g - 1
        if 0 <= t < 16:
            pairs += [(g * 4 + z, t * 4 + 3 - z) for z in range(4)]
    return pairs


def group_index():
    return (lax.axis_index("x") * 2 + lax.axis_index("zh")) * 2 + lax.axis_index("core")


def row_of(block):
    return ((block >> 4) << 3) + (block & 7)


def parity_of(block):
    return (block >> 3) & 1


def terms_kernel(columns, lower, upper, adj, tiles, sums, give_off, on):
    odd, mine = lax.axis_index("core"), lax.axis_index("yp")
    off_base = GROUP_BLOCKS + HALO * odd
    on_base = GROUP_BLOCKS + HALO * (1 - odd)
    for i in range(ROWS):
        sums[i] = jnp.zeros(PLANES, jnp.float32)
    for b in range(2):
        rows = adj[b]
        for k in range(17):
            term = jnp.dot(rows, tiles[k, b], preferred_element_type=jnp.float32)
            tail = jnp.concatenate([term[:16, 128:], term[16:, 128:]], axis=1)
            planes = jnp.concatenate([term[:16, :128], term[16:, :128], tail], axis=0)
            if k == 0:
                target = lax.axis_index("yh") * 8 + lax.axis_index("zl") * 2 + b
            else:
                c = columns[b, k - 1]
                slot = c - off_base
                target = jnp.where(
                    c < GROUP_BLOCKS,
                    ((parity_of(c) ^ mine) << 5) + row_of(c),
                    jnp.where(
                        (slot >= 0) & (slot < HALO),
                        OFF + (((slot >> 4) ^ mine) << 4) + (slot & 15),
                        ON + c - on_base,
                    ),
                )
            sums[target] += planes
    give_off[...] = sums[OFF + 16 : OFF + 32]
    on[...] = sums[ON : ON + HALO]


def merge_kernel(lower, upper, got_off, got_on, own, own_off, keep, give, leaving):
    sibling, odd = group_index() ^ 1, lax.axis_index("core")
    mine = lax.axis_index("yp")
    leaving[...] = own_off[...] + got_off[...]
    keep[...] = own[KEEP : KEEP + 32]
    give[...] = own[GIVE : GIVE + 32]
    for h in range(HALO):
        block = jnp.where(odd == 1, upper[sibling, h], lower[sibling, h])
        same = parity_of(block) == mine
        row = row_of(block)

        @pl.when(same)
        def _():
            keep[row] += got_on[h]

        @pl.when(jnp.logical_not(same))
        def _():
            give[row] += got_on[h]


def place_kernel(lower, upper, keep, got, crossed, passed, out):
    group, odd = group_index(), lax.axis_index("core")
    mine = lax.axis_index("yp")
    above = jnp.minimum(group + 1, lower.shape[0] - 1)
    below = jnp.maximum(group - 1, 0)
    out[...] = keep[...] + got[...]
    for i in range(16):
        for source, half in ((crossed, mine), (passed, 1 - mine)):
            slot = half * 16 + i
            block = jnp.where(odd == 1, lower[above, slot], upper[below, slot])
            row = row_of(block)

            @pl.when(parity_of(block) == mine)
            def _():
                out[row] += source[i]


def spectral_kernel(matrix, adj, rates, out):
    for b in range(2):
        part = jnp.dot(
            matrix[...],
            adj[b].astype(jnp.float32),
            precision=lax.Precision.HIGHEST,
            preferred_element_type=jnp.float32,
        )
        out[b] = rates[b : b + 1, :] * part


def last_kernel(shared, part, precond, out):
    for b in range(2):
        total = shared[0, b]
        for i in range(1, 16):
            total += shared[i, b]
        tail = total[32:48]
        top = jnp.concatenate([total[:16], tail[:, :64]], axis=1)
        bottom = jnp.concatenate([total[16:32], tail[:, 64:]], axis=1)
        combined = (jnp.concatenate([top, bottom], axis=0) + part[b]).astype(jnp.bfloat16)
        out[b] = jnp.dot(combined, precond[b], preferred_element_type=jnp.float32).astype(
            jnp.bfloat16
        )


def whole():
    return pl.BlockSpec(memory_space=pltpu.VMEM)


def scalars():
    return pl.BlockSpec(memory_space=pltpu.SMEM)


def blocks_of(count, start):
    return pl.BlockSpec((count,) + PLANES, lambda i: (start // count, 0, 0))


def stack(*counts):
    return [jax.ShapeDtypeStruct((n,) + PLANES, jnp.float32) for n in counts]


def shards(adjoint, jacobian_tiles, columns, cell_rates, precond, lower_list, upper_list):
    blocks, row_count, tile_width = adjoint.shape
    slots = jacobian_tiles.shape[1]
    tiles = jacobian_tiles.reshape(blocks, slots, tile_width, tile_width).transpose(1, 0, 2, 3)
    square_precond = precond.reshape(blocks, tile_width, tile_width)
    padded = jnp.pad(
        adjoint.reshape(blocks, ADJ, INST, tile_width), ((0, 0), (0, 0), (0, 1), (0, 0))
    ).reshape(blocks, 32, tile_width)

    sums, give_off, on = pl.pallas_call(
        terms_kernel,
        out_shape=stack(ROWS, 16, HALO),
        in_specs=[scalars(), scalars(), scalars(), whole(), whole()],
        out_specs=[whole()] * 3,
        compiler_params=pltpu.CompilerParams(vmem_limit_bytes=32 * 2**20),
        name="terms",
    )(columns, lower_list, upper_list, padded, tiles)
    got_off = to_mate(give_off)
    got_on = lax.ppermute(on, "core", [(0, 1), (1, 0)])
    keep, give, leaving = pl.pallas_call(
        merge_kernel,
        out_shape=stack(32, 32, 16),
        grid=(1,),
        in_specs=[scalars(), scalars(), blocks_of(16, 0), blocks_of(HALO, 0)]
        + [blocks_of(64, KEEP), blocks_of(16, OFF)],
        out_specs=[blocks_of(n, 0) for n in (32, 32, 16)],
        compiler_params=pltpu.CompilerParams(vmem_limit_bytes=24 * 2**20),
        name="merge",
    )(lower_list, upper_list, got_off, got_on, sums, sums)
    crossed = lax.ppermute(leaving, ("x", "zh", "core", "zl"), off_chip_pairs())
    got = to_mate(give)
    passed = to_mate(crossed)
    merged = pl.pallas_call(
        place_kernel,
        out_shape=stack(32)[0],
        grid=(1,),
        in_specs=[scalars(), scalars()] + [blocks_of(n, 0) for n in (32, 32, 16, 16)],
        out_specs=blocks_of(32, 0),
        compiler_params=pltpu.CompilerParams(vmem_limit_bytes=16 * 2**20),
        name="place",
    )(lower_list, upper_list, keep, got, crossed, passed)
    shared = lax.all_to_all(merged.reshape(16, -1), ("yh", "zl"), 0, 0, tiled=True)

    half = jnp.pad(spectral_matrix(INST).T, ((0, 1), (0, 1)))
    matrix = jnp.kron(jnp.eye(ADJ, dtype=jnp.float32), half)
    part = pl.pallas_call(
        spectral_kernel,
        out_shape=jax.ShapeDtypeStruct((blocks, 32, tile_width), jnp.float32),
        in_specs=[whole()] * 3,
        out_specs=whole(),
        compiler_params=pltpu.CompilerParams(vmem_limit_bytes=8 * 2**20),
        name="spectral",
    )(matrix, padded, cell_rates)
    result = pl.pallas_call(
        last_kernel,
        out_shape=jax.ShapeDtypeStruct((blocks, 32, tile_width), jnp.bfloat16),
        in_specs=[whole()] * 3,
        out_specs=whole(),
        compiler_params=pltpu.CompilerParams(vmem_limit_bytes=8 * 2**20),
        name="last",
    )(shared.reshape(16, blocks, *PLANES), part, square_precond)
    return (
        result.reshape(blocks, ADJ, 16, tile_width)[:, :, :INST]
        .reshape(blocks, row_count, tile_width)
    )


def solution(mesh):
    split_mesh = Mesh(mesh.devices.reshape(SIZES), AXES)
    split = P(AXES)
    return jax.shard_map(
        shards,
        mesh=split_mesh,
        in_specs=(split, split, split, split, split, P(), P()),
        out_specs=split,
        check_vma=False,
    )
```

```python
import jax
import jax.numpy as jnp
from jax import lax
from jax.experimental import pallas as pl
from jax.experimental.pallas import tpu as pltpu
from jax.sharding import Mesh, PartitionSpec as P

INST = 15
ADJ = 2
HALO = 32
GROUP_BLOCKS = 64
AXES = ("x", "zh", "core", "yh", "yp", "zq", "zp")
SIZES = (4, 2, 2, 4, 2, 2, 2)
PLANES = (48, 128)
KEEP, GIVE, OFF, ON, ROWS = 0, 32, 64, 96, 128


def spectral_matrix(length):
    row_index = jnp.arange(length)[:, None]
    col_index = jnp.arange(length)[None, :]
    offset = row_index - col_index
    parity = jnp.where(offset % 2 == 0, 1.0, -1.0).astype(jnp.float32)
    phase_angle = jnp.pi / length * offset.astype(jnp.float32)
    sine_values = jnp.where(offset == 0, 1.0, jnp.sin(phase_angle))
    return jnp.where(offset == 0, 0.0, 0.5 * parity / sine_values)


def mate_of(core, y):
    return ((((y - core) % 8) ^ 1) + core) % 8


def to_mate(value):
    pairs = [(c * 8 + y, c * 8 + mate_of(c, y)) for c in range(2) for y in range(8)]
    return lax.ppermute(value, ("core", "yh", "yp"), pairs)


def to_side(value):
    return lax.ppermute(value, "zp", [(0, 1), (1, 0)])


def to_mates_side(value):
    pairs = [
        (c * 16 + y * 2 + z, c * 16 + mate_of(c, y) * 2 + 1 - z)
        for c in range(2)
        for y in range(8)
        for z in range(2)
    ]
    return lax.ppermute(value, ("core", "yh", "yp", "zp"), pairs)


def off_chip_pairs():
    pairs = []
    for g in range(16):
        t = g + 1 if g % 2 else g - 1
        if 0 <= t < 16:
            pairs += [(g * 4 + z, t * 4 + 3 - z) for z in range(4)]
    return pairs


def group_index():
    return (lax.axis_index("x") * 2 + lax.axis_index("zh")) * 2 + lax.axis_index("core")


def row_of(block):
    return ((block >> 4) << 3) + (block & 7)


def parity_of(block):
    return (block >> 3) & 1


def terms_kernel(columns, lower, upper, adj, tiles, sums, side, mate, cross, on):
    odd, mine = lax.axis_index("core"), lax.axis_index("yp")
    quarter = mine * 2 + lax.axis_index("zp")
    off_base = GROUP_BLOCKS + HALO * odd
    on_base = GROUP_BLOCKS + HALO * (1 - odd)
    for i in range(ROWS):
        sums[i] = jnp.zeros(PLANES, jnp.float32)
    for b in range(2):
        rows = adj[b]
        for k in range(17):
            term = jnp.dot(rows, tiles[k, b], preferred_element_type=jnp.float32)
            tail = jnp.concatenate([term[:16, 128:], term[16:, 128:]], axis=1)
            planes = jnp.concatenate([term[:16, :128], term[16:, :128], tail], axis=0)
            if k == 0:
                target = lax.axis_index("yh") * 8 + lax.axis_index("zq") * 4 + lax.axis_index("zp") * 2 + b
            else:
                c = columns[b, k - 1]
                slot = c - off_base
                target = jnp.where(
                    c < GROUP_BLOCKS,
                    ((parity_of(c) ^ mine) << 5) + row_of(c),
                    jnp.where(
                        (slot >= 0) & (slot < HALO),
                        OFF + (((slot >> 3) ^ quarter) << 3) + (slot & 7),
                        ON + c - on_base,
                    ),
                )
            sums[target] += planes
    side[...] = sums[OFF + 8 : OFF + 16]
    mate[...] = sums[OFF + 16 : OFF + 24]
    cross[...] = sums[OFF + 24 : OFF + 32]
    on[...] = sums[ON : ON + HALO]


def merge_kernel(lower, upper, side, mate, cross, got_on, sums, keep, give, leaving):
    sibling, odd = group_index() ^ 1, lax.axis_index("core")
    mine = lax.axis_index("yp")
    leaving[...] = (sums[OFF : OFF + 8] + side[...]) + (mate[...] + cross[...])
    keep[...] = sums[KEEP : KEEP + 32]
    give[...] = sums[GIVE : GIVE + 32]
    for h in range(HALO):
        block = jnp.where(odd == 1, upper[sibling, h], lower[sibling, h])
        same = parity_of(block) == mine
        row = row_of(block)

        @pl.when(same)
        def _():
            keep[row] += got_on[h]

        @pl.when(jnp.logical_not(same))
        def _():
            give[row] += got_on[h]


def place_kernel(lower, upper, keep, got, crossed, passed, out):
    group, odd = group_index(), lax.axis_index("core")
    mine = lax.axis_index("yp")
    above = jnp.minimum(group + 1, lower.shape[0] - 1)
    below = jnp.maximum(group - 1, 0)
    out[...] = keep[...] + got[...]
    mirrored = 1 - lax.axis_index("zp")
    for i in range(8):
        for source, parity in ((crossed, mine), (passed, 1 - mine)):
            slot = parity * 16 + mirrored * 8 + i
            block = jnp.where(odd == 1, lower[above, slot], upper[below, slot])
            row = row_of(block)

            @pl.when(parity_of(block) == mine)
            def _():
                out[row] += source[i]


def spectral_kernel(matrix, adj, rates, out):
    for b in range(2):
        part = jnp.dot(
            matrix[...],
            adj[b].astype(jnp.float32),
            precision=lax.Precision.HIGHEST,
            preferred_element_type=jnp.float32,
        )
        out[b] = rates[b : b + 1, :] * part


def last_kernel(shared, part, precond, out):
    for b in range(2):
        total = shared[0, b]
        for i in range(1, 16):
            total += shared[i, b]
        tail = total[32:48]
        top = jnp.concatenate([total[:16], tail[:, :64]], axis=1)
        bottom = jnp.concatenate([total[16:32], tail[:, 64:]], axis=1)
        combined = (jnp.concatenate([top, bottom], axis=0) + part[b]).astype(jnp.bfloat16)
        out[b] = jnp.dot(combined, precond[b], preferred_element_type=jnp.float32).astype(
            jnp.bfloat16
        )


def whole():
    return pl.BlockSpec(memory_space=pltpu.VMEM)


def scalars():
    return pl.BlockSpec(memory_space=pltpu.SMEM)


def stack(*counts):
    return [jax.ShapeDtypeStruct((n,) + PLANES, jnp.float32) for n in counts]


def shards(adjoint, jacobian_tiles, columns, cell_rates, precond, lower_list, upper_list):
    blocks, row_count, tile_width = adjoint.shape
    slots = jacobian_tiles.shape[1]
    tiles = jacobian_tiles.reshape(blocks, slots, tile_width, tile_width).transpose(1, 0, 2, 3)
    square_precond = precond.reshape(blocks, tile_width, tile_width)
    padded = jnp.pad(
        adjoint.reshape(blocks, ADJ, INST, tile_width), ((0, 0), (0, 0), (0, 1), (0, 0))
    ).reshape(blocks, 32, tile_width)

    sums, side, mate, cross, on = pl.pallas_call(
        terms_kernel,
        out_shape=stack(ROWS, 8, 8, 8, HALO),
        in_specs=[scalars(), scalars(), scalars(), whole(), whole()],
        out_specs=[whole()] * 5,
        compiler_params=pltpu.CompilerParams(vmem_limit_bytes=32 * 2**20),
        name="terms",
    )(columns, lower_list, upper_list, padded, tiles)
    side, mate, cross = to_side(side), to_mate(mate), to_mates_side(cross)
    got_on = lax.ppermute(on, "core", [(0, 1), (1, 0)])
    keep, give, leaving = pl.pallas_call(
        merge_kernel,
        out_shape=stack(32, 32, 8),
        in_specs=[scalars(), scalars()] + [whole()] * 5,
        out_specs=[whole()] * 3,
        compiler_params=pltpu.CompilerParams(vmem_limit_bytes=24 * 2**20),
        name="merge",
    )(lower_list, upper_list, side, mate, cross, got_on, sums)
    crossed = lax.ppermute(leaving, ("x", "zh", "core", "zq", "zp"), off_chip_pairs())
    got = to_mate(give)
    passed = to_mate(crossed)
    merged = pl.pallas_call(
        place_kernel,
        out_shape=stack(32)[0],
        in_specs=[scalars(), scalars()] + [whole()] * 4,
        out_specs=whole(),
        compiler_params=pltpu.CompilerParams(vmem_limit_bytes=16 * 2**20),
        name="place",
    )(lower_list, upper_list, keep, got, crossed, passed)
    shared = lax.all_to_all(merged.reshape(16, -1), ("yh", "zq", "zp"), 0, 0, tiled=True)

    half = jnp.pad(spectral_matrix(INST).T, ((0, 1), (0, 1)))
    matrix = jnp.kron(jnp.eye(ADJ, dtype=jnp.float32), half)
    part = pl.pallas_call(
        spectral_kernel,
        out_shape=jax.ShapeDtypeStruct((blocks, 32, tile_width), jnp.float32),
        in_specs=[whole()] * 3,
        out_specs=whole(),
        compiler_params=pltpu.CompilerParams(vmem_limit_bytes=8 * 2**20),
        name="spectral",
    )(matrix, padded, cell_rates)
    result = pl.pallas_call(
        last_kernel,
        out_shape=jax.ShapeDtypeStruct((blocks, 32, tile_width), jnp.bfloat16),
        in_specs=[whole()] * 3,
        out_specs=whole(),
        compiler_params=pltpu.CompilerParams(vmem_limit_bytes=8 * 2**20),
        name="last",
    )(shared.reshape(16, blocks, *PLANES), part, square_precond)
    return (
        result.reshape(blocks, ADJ, 16, tile_width)[:, :, :INST]
        .reshape(blocks, row_count, tile_width)
    )


def solution(mesh):
    split_mesh = Mesh(mesh.devices.reshape(SIZES), AXES)
    split = P(AXES)
    return jax.shard_map(
        shards,
        mesh=split_mesh,
        in_specs=(split, split, split, split, split, P(), P()),
        out_specs=split,
        check_vma=False,
    )
```

```python
import jax
import jax.numpy as jnp
from jax import lax
from jax.experimental import pallas as pl
from jax.experimental.pallas import tpu as pltpu
from jax.sharding import Mesh, PartitionSpec as P

INST = 15
ADJ = 2
HALO = 32
GROUP_BLOCKS = 64
AXES = ("x", "zh", "core", "yh", "yp", "zl")
SIZES = (4, 2, 2, 4, 2, 4)
PLANES = (48, 128)
KEEP, GIVE, OFF_KEEP, OFF_GIVE, ON, ROWS = 0, 32, 64, 96, 128, 160


def spectral_matrix(length):
    row_index = jnp.arange(length)[:, None]
    col_index = jnp.arange(length)[None, :]
    offset = row_index - col_index
    parity = jnp.where(offset % 2 == 0, 1.0, -1.0).astype(jnp.float32)
    phase_angle = jnp.pi / length * offset.astype(jnp.float32)
    sine_values = jnp.where(offset == 0, 1.0, jnp.sin(phase_angle))
    return jnp.where(offset == 0, 0.0, 0.5 * parity / sine_values)


def mate_of(core, y):
    return ((((y - core) % 8) ^ 1) + core) % 8


def to_mate(value):
    pairs = [(c * 8 + y, c * 8 + mate_of(c, y)) for c in range(2) for y in range(8)]
    return lax.ppermute(value, ("core", "yh", "yp"), pairs)


def off_chip_pairs():
    pairs = []
    for g in range(16):
        t = g + 1 if g % 2 else g - 1
        if 0 <= t < 16:
            pairs += [(g * 4 + z, t * 4 + z) for z in range(4)]
    return pairs


def group_index():
    return (lax.axis_index("x") * 2 + lax.axis_index("zh")) * 2 + lax.axis_index("core")


def row_of(block):
    return ((block >> 4) << 3) + (block & 7)


def parity_of(block):
    return (block >> 3) & 1


def terms_kernel(columns, lower, upper, adj, tiles, sums, give_off, on):
    group, odd, mine = group_index(), lax.axis_index("core"), lax.axis_index("yp")
    off_base = GROUP_BLOCKS + HALO * odd
    on_base = GROUP_BLOCKS + HALO * (1 - odd)

    def place(block):
        return ((parity_of(block) ^ mine) << 5) + row_of(block)

    for i in range(ROWS):
        sums[i] = jnp.zeros(PLANES, jnp.float32)
    for b in range(2):
        rows = adj[b]
        for k in range(17):
            term = jnp.dot(rows, tiles[k, b], preferred_element_type=jnp.float32)
            tail = jnp.concatenate([term[:16, 128:], term[16:, 128:]], axis=1)
            planes = jnp.concatenate([term[:16, :128], term[16:, :128], tail], axis=0)
            if k == 0:
                target = lax.axis_index("yh") * 8 + lax.axis_index("zl") * 2 + b
            else:
                c = columns[b, k - 1]
                slot = jnp.clip(c - off_base, 0, HALO - 1)
                away = jnp.where(odd == 1, upper[group, slot], lower[group, slot])
                target = jnp.where(
                    c < GROUP_BLOCKS,
                    KEEP + place(c),
                    jnp.where(
                        (c >= off_base) & (c < off_base + HALO),
                        OFF_KEEP + place(away),
                        ON + c - on_base,
                    ),
                )
            sums[target] += planes
    give_off[...] = sums[OFF_GIVE : OFF_GIVE + 32]
    on[...] = sums[ON : ON + HALO]


def merge_kernel(lower, upper, got_off, got_on, sums, keep, give, leaving):
    sibling, odd = group_index() ^ 1, lax.axis_index("core")
    mine = lax.axis_index("yp")
    leaving[...] = sums[OFF_KEEP : OFF_KEEP + 32] + got_off[...]
    keep[...] = sums[KEEP : KEEP + 32]
    give[...] = sums[GIVE : GIVE + 32]
    for h in range(HALO):
        block = jnp.where(odd == 1, upper[sibling, h], lower[sibling, h])
        same = parity_of(block) == mine
        row = row_of(block)

        @pl.when(same)
        def _():
            keep[row] += got_on[h]

        @pl.when(jnp.logical_not(same))
        def _():
            give[row] += got_on[h]


def spectral_kernel(matrix, adj, rates, out):
    for b in range(2):
        part = jnp.dot(
            matrix[...],
            adj[b].astype(jnp.float32),
            precision=lax.Precision.HIGHEST,
            preferred_element_type=jnp.float32,
        )
        out[b] = rates[b : b + 1, :] * part


def last_kernel(shared, crossed, part, precond, out):
    for b in range(2):
        total = shared[0, b]
        for i in range(1, 16):
            total += shared[i, b]
        total += crossed[b]
        tail = total[32:48]
        top = jnp.concatenate([total[:16], tail[:, :64]], axis=1)
        bottom = jnp.concatenate([total[16:32], tail[:, 64:]], axis=1)
        combined = (jnp.concatenate([top, bottom], axis=0) + part[b]).astype(jnp.bfloat16)
        out[b] = jnp.dot(combined, precond[b], preferred_element_type=jnp.float32).astype(
            jnp.bfloat16
        )


def whole():
    return pl.BlockSpec(memory_space=pltpu.VMEM)


def scalars():
    return pl.BlockSpec(memory_space=pltpu.SMEM)


def stack(*counts):
    return [jax.ShapeDtypeStruct((n,) + PLANES, jnp.float32) for n in counts]


def shards(adjoint, jacobian_tiles, columns, cell_rates, precond, lower_list, upper_list):
    blocks, row_count, tile_width = adjoint.shape
    slots = jacobian_tiles.shape[1]
    tiles = jacobian_tiles.reshape(blocks, slots, tile_width, tile_width).transpose(1, 0, 2, 3)
    square_precond = precond.reshape(blocks, tile_width, tile_width)
    padded = jnp.pad(
        adjoint.reshape(blocks, ADJ, INST, tile_width), ((0, 0), (0, 0), (0, 1), (0, 0))
    ).reshape(blocks, 32, tile_width)

    sums, give_off, on = pl.pallas_call(
        terms_kernel,
        out_shape=stack(ROWS, 32, HALO),
        in_specs=[scalars(), scalars(), scalars(), whole(), whole()],
        out_specs=[whole()] * 3,
        compiler_params=pltpu.CompilerParams(vmem_limit_bytes=32 * 2**20),
        name="terms",
    )(columns, lower_list, upper_list, padded, tiles)
    got_off = to_mate(give_off)
    got_on = lax.ppermute(on, "core", [(0, 1), (1, 0)])
    keep, give, leaving = pl.pallas_call(
        merge_kernel,
        out_shape=stack(32, 32, 32),
        in_specs=[scalars(), scalars()] + [whole()] * 3,
        out_specs=[whole()] * 3,
        compiler_params=pltpu.CompilerParams(vmem_limit_bytes=24 * 2**20),
        name="merge",
    )(lower_list, upper_list, got_off, got_on, sums)
    got = to_mate(give)
    off_shared = lax.all_to_all(leaving.reshape(16, -1), ("yh", "zl"), 0, 0, tiled=True)
    shared = lax.all_to_all((keep + got).reshape(16, -1), ("yh", "zl"), 0, 0, tiled=True)
    finished = jnp.sum(off_shared.reshape(16, blocks, *PLANES), axis=0)
    crossed = lax.ppermute(finished, ("x", "zh", "core", "zl"), off_chip_pairs())

    half = jnp.pad(spectral_matrix(INST).T, ((0, 1), (0, 1)))
    matrix = jnp.kron(jnp.eye(ADJ, dtype=jnp.float32), half)
    part = pl.pallas_call(
        spectral_kernel,
        out_shape=jax.ShapeDtypeStruct((blocks, 32, tile_width), jnp.float32),
        in_specs=[whole()] * 3,
        out_specs=whole(),
        compiler_params=pltpu.CompilerParams(vmem_limit_bytes=8 * 2**20),
        name="spectral",
    )(matrix, padded, cell_rates)
    result = pl.pallas_call(
        last_kernel,
        out_shape=jax.ShapeDtypeStruct((blocks, 32, tile_width), jnp.bfloat16),
        in_specs=[whole()] * 4,
        out_specs=whole(),
        compiler_params=pltpu.CompilerParams(vmem_limit_bytes=8 * 2**20),
        name="last",
    )(shared.reshape(16, blocks, *PLANES), crossed, part, square_precond)
    return (
        result.reshape(blocks, ADJ, 16, tile_width)[:, :, :INST]
        .reshape(blocks, row_count, tile_width)
    )


def solution(mesh):
    split_mesh = Mesh(mesh.devices.reshape(SIZES), AXES)
    split = P(AXES)
    return jax.shard_map(
        shards,
        mesh=split_mesh,
        in_specs=(split, split, split, split, split, P(), P()),
        out_specs=split,
        check_vma=False,
    )
```

```python
import jax
import jax.numpy as jnp
from jax import lax
from jax.experimental import pallas as pl
from jax.experimental.pallas import tpu as pltpu
from jax.sharding import Mesh, PartitionSpec as P

INST = 15
ADJ = 2
HALO = 32
GROUP_BLOCKS = 64
AXES = ("x", "zh", "core", "yh", "yp", "zq", "zp")
SIZES = (4, 2, 2, 4, 2, 2, 2)
PLANES = (48, 128)
KEEP, GIVE, OFF, ON, ROWS = 0, 32, 64, 96, 128


def spectral_matrix(length):
    row_index = jnp.arange(length)[:, None]
    col_index = jnp.arange(length)[None, :]
    offset = row_index - col_index
    parity = jnp.where(offset % 2 == 0, 1.0, -1.0).astype(jnp.float32)
    phase_angle = jnp.pi / length * offset.astype(jnp.float32)
    sine_values = jnp.where(offset == 0, 1.0, jnp.sin(phase_angle))
    return jnp.where(offset == 0, 0.0, 0.5 * parity / sine_values)


def mate_of(core, y):
    return ((((y - core) % 8) ^ 1) + core) % 8


def to_mate(value):
    pairs = [(c * 8 + y, c * 8 + mate_of(c, y)) for c in range(2) for y in range(8)]
    return lax.ppermute(value, ("core", "yh", "yp"), pairs)


def to_side(value):
    return lax.ppermute(value, "zp", [(0, 1), (1, 0)])


def to_mates_side(value):
    pairs = [
        (c * 16 + y * 2 + z, c * 16 + mate_of(c, y) * 2 + 1 - z)
        for c in range(2)
        for y in range(8)
        for z in range(2)
    ]
    return lax.ppermute(value, ("core", "yh", "yp", "zp"), pairs)


def off_chip_pairs():
    pairs = []
    for g in range(16):
        t = g + 1 if g % 2 else g - 1
        if 0 <= t < 16:
            pairs += [(g * 4 + z, t * 4 + 3 - z) for z in range(4)]
    return pairs


def group_index():
    return (lax.axis_index("x") * 2 + lax.axis_index("zh")) * 2 + lax.axis_index("core")


def row_of(block):
    return ((block >> 4) << 3) + (block & 7)


def parity_of(block):
    return (block >> 3) & 1


def terms_kernel(columns, lower, upper, adj, tiles, sums, own, side, mate, cross, on):
    odd, mine = lax.axis_index("core"), lax.axis_index("yp")
    quarter = mine * 2 + lax.axis_index("zp")
    off_base = GROUP_BLOCKS + HALO * odd
    on_base = GROUP_BLOCKS + HALO * (1 - odd)
    for i in range(ROWS):
        sums[i] = jnp.zeros(PLANES, jnp.float32)
    for b in range(2):
        rows = adj[b]
        for k in range(17):
            term = jnp.dot(rows, tiles[k, b], preferred_element_type=jnp.float32)
            tail = jnp.concatenate([term[:16, 128:], term[16:, 128:]], axis=1)
            planes = jnp.concatenate([term[:16, :128], term[16:, :128], tail], axis=0)
            if k == 0:
                target = lax.axis_index("yh") * 8 + lax.axis_index("zq") * 4 + lax.axis_index("zp") * 2 + b
            else:
                c = columns[b, k - 1]
                slot = c - off_base
                target = jnp.where(
                    c < GROUP_BLOCKS,
                    ((parity_of(c) ^ mine) << 5) + row_of(c),
                    jnp.where(
                        (slot >= 0) & (slot < HALO),
                        OFF + (((slot >> 3) ^ quarter) << 3) + (slot & 7),
                        ON + c - on_base,
                    ),
                )
            sums[target] += planes
    own[...] = sums[OFF : OFF + 8]
    side[...] = sums[OFF + 8 : OFF + 16]
    mate[...] = sums[OFF + 16 : OFF + 24]
    cross[...] = sums[OFF + 24 : OFF + 32]
    on[...] = sums[ON : ON + HALO]


def quarter_kernel(side, mate, cross, own, leaving):
    leaving[...] = (own[...] + side[...]) + (mate[...] + cross[...])


def merge_kernel(lower, upper, got_on, sums, keep, give):
    sibling, odd = group_index() ^ 1, lax.axis_index("core")
    mine = lax.axis_index("yp")
    keep[...] = sums[KEEP : KEEP + 32]
    give[...] = sums[GIVE : GIVE + 32]
    for h in range(HALO):
        block = jnp.where(odd == 1, upper[sibling, h], lower[sibling, h])
        same = parity_of(block) == mine
        row = row_of(block)

        @pl.when(same)
        def _():
            keep[row] += got_on[h]

        @pl.when(jnp.logical_not(same))
        def _():
            give[row] += got_on[h]


def place_kernel(lower, upper, keep, got, crossed, passed, out):
    group, odd = group_index(), lax.axis_index("core")
    mine = lax.axis_index("yp")
    above = jnp.minimum(group + 1, lower.shape[0] - 1)
    below = jnp.maximum(group - 1, 0)
    out[...] = keep[...] + got[...]
    mirrored = 1 - lax.axis_index("zp")
    for i in range(8):
        for source, parity in ((crossed, mine), (passed, 1 - mine)):
            slot = parity * 16 + mirrored * 8 + i
            block = jnp.where(odd == 1, lower[above, slot], upper[below, slot])
            row = row_of(block)

            @pl.when(parity_of(block) == mine)
            def _():
                out[row] += source[i]


def spectral_kernel(matrix, adj, rates, out):
    for b in range(2):
        part = jnp.dot(
            matrix[...],
            adj[b].astype(jnp.float32),
            precision=lax.Precision.HIGHEST,
            preferred_element_type=jnp.float32,
        )
        out[b] = rates[b : b + 1, :] * part


def last_kernel(shared, part, precond, out):
    for b in range(2):
        total = shared[0, b]
        for i in range(1, 16):
            total += shared[i, b]
        tail = total[32:48]
        top = jnp.concatenate([total[:16], tail[:, :64]], axis=1)
        bottom = jnp.concatenate([total[16:32], tail[:, 64:]], axis=1)
        combined = (jnp.concatenate([top, bottom], axis=0) + part[b]).astype(jnp.bfloat16)
        out[b] = jnp.dot(combined, precond[b], preferred_element_type=jnp.float32).astype(
            jnp.bfloat16
        )


def whole():
    return pl.BlockSpec(memory_space=pltpu.VMEM)


def scalars():
    return pl.BlockSpec(memory_space=pltpu.SMEM)


def stack(*counts):
    return [jax.ShapeDtypeStruct((n,) + PLANES, jnp.float32) for n in counts]


def shards(adjoint, jacobian_tiles, columns, cell_rates, precond, lower_list, upper_list):
    blocks, row_count, tile_width = adjoint.shape
    slots = jacobian_tiles.shape[1]
    tiles = jacobian_tiles.reshape(blocks, slots, tile_width, tile_width).transpose(1, 0, 2, 3)
    square_precond = precond.reshape(blocks, tile_width, tile_width)
    padded = jnp.pad(
        adjoint.reshape(blocks, ADJ, INST, tile_width), ((0, 0), (0, 0), (0, 1), (0, 0))
    ).reshape(blocks, 32, tile_width)

    sums, own, side, mate, cross, on = pl.pallas_call(
        terms_kernel,
        out_shape=stack(ROWS, 8, 8, 8, 8, HALO),
        in_specs=[scalars(), scalars(), scalars(), whole(), whole()],
        out_specs=[whole()] * 6,
        compiler_params=pltpu.CompilerParams(vmem_limit_bytes=32 * 2**20),
        name="terms",
    )(columns, lower_list, upper_list, padded, tiles)
    leaving = pl.pallas_call(
        quarter_kernel,
        out_shape=stack(8)[0],
        in_specs=[whole()] * 4,
        out_specs=whole(),
        compiler_params=pltpu.CompilerParams(vmem_limit_bytes=16 * 2**20),
        name="quarter",
    )(to_side(side), to_mate(mate), to_mates_side(cross), own)
    leaving, on = lax.optimization_barrier((leaving, on))
    crossed = lax.ppermute(leaving, ("x", "zh", "core", "zq", "zp"), off_chip_pairs())
    got_on = lax.ppermute(on, "core", [(0, 1), (1, 0)])
    keep, give = pl.pallas_call(
        merge_kernel,
        out_shape=stack(32, 32),
        in_specs=[scalars(), scalars()] + [whole()] * 2,
        out_specs=[whole()] * 2,
        compiler_params=pltpu.CompilerParams(vmem_limit_bytes=24 * 2**20),
        name="merge",
    )(lower_list, upper_list, got_on, sums)
    got = to_mate(give)
    passed = to_mate(crossed)
    merged = pl.pallas_call(
        place_kernel,
        out_shape=stack(32)[0],
        in_specs=[scalars(), scalars()] + [whole()] * 4,
        out_specs=whole(),
        compiler_params=pltpu.CompilerParams(vmem_limit_bytes=16 * 2**20),
        name="place",
    )(lower_list, upper_list, keep, got, crossed, passed)
    shared = lax.all_to_all(merged.reshape(16, -1), ("yh", "zq", "zp"), 0, 0, tiled=True)

    half = jnp.pad(spectral_matrix(INST).T, ((0, 1), (0, 1)))
    matrix = jnp.kron(jnp.eye(ADJ, dtype=jnp.float32), half)
    part = pl.pallas_call(
        spectral_kernel,
        out_shape=jax.ShapeDtypeStruct((blocks, 32, tile_width), jnp.float32),
        in_specs=[whole()] * 3,
        out_specs=whole(),
        compiler_params=pltpu.CompilerParams(vmem_limit_bytes=8 * 2**20),
        name="spectral",
    )(matrix, padded, cell_rates)
    result = pl.pallas_call(
        last_kernel,
        out_shape=jax.ShapeDtypeStruct((blocks, 32, tile_width), jnp.bfloat16),
        in_specs=[whole()] * 3,
        out_specs=whole(),
        compiler_params=pltpu.CompilerParams(vmem_limit_bytes=8 * 2**20),
        name="last",
    )(shared.reshape(16, blocks, *PLANES), part, square_precond)
    return (
        result.reshape(blocks, ADJ, 16, tile_width)[:, :, :INST]
        .reshape(blocks, row_count, tile_width)
    )


def solution(mesh):
    split_mesh = Mesh(mesh.devices.reshape(SIZES), AXES)
    split = P(AXES)
    return jax.shard_map(
        shards,
        mesh=split_mesh,
        in_specs=(split, split, split, split, split, P(), P()),
        out_specs=split,
        check_vma=False,
    )
```

```python
import jax
import jax.numpy as jnp
from jax import lax
from jax.experimental import pallas as pl
from jax.experimental.pallas import tpu as pltpu
from jax.sharding import Mesh, PartitionSpec as P

INST = 15
ADJ = 2
HALO = 32
GROUP_BLOCKS = 64
AXES = ("x", "zh", "core", "yh", "yp", "zq", "zp")
SIZES = (4, 2, 2, 4, 2, 2, 2)
PLANES = (48, 128)
TILE = 192
LANE_PARTS = ((0, 0), (1, 0), (1, 1), (2, 1))
KEEP, GIVE, OFF, ON, ROWS = 0, 32, 64, 96, 128


def spectral_matrix(length):
    row_index = jnp.arange(length)[:, None]
    col_index = jnp.arange(length)[None, :]
    offset = row_index - col_index
    parity = jnp.where(offset % 2 == 0, 1.0, -1.0).astype(jnp.float32)
    phase_angle = jnp.pi / length * offset.astype(jnp.float32)
    sine_values = jnp.where(offset == 0, 1.0, jnp.sin(phase_angle))
    return jnp.where(offset == 0, 0.0, 0.5 * parity / sine_values)


def mate_of(core, y):
    return ((((y - core) % 8) ^ 1) + core) % 8


def to_mate(value):
    pairs = [(c * 8 + y, c * 8 + mate_of(c, y)) for c in range(2) for y in range(8)]
    return lax.ppermute(value, ("core", "yh", "yp"), pairs)


def to_side(value):
    return lax.ppermute(value, "zp", [(0, 1), (1, 0)])


def to_mates_side(value):
    pairs = [
        (c * 16 + y * 2 + z, c * 16 + mate_of(c, y) * 2 + 1 - z)
        for c in range(2)
        for y in range(8)
        for z in range(2)
    ]
    return lax.ppermute(value, ("core", "yh", "yp", "zp"), pairs)


def off_chip_pairs():
    pairs = []
    for g in range(16):
        t = g + 1 if g % 2 else g - 1
        if 0 <= t < 16:
            pairs += [(g * 4 + z, t * 4 + 3 - z) for z in range(4)]
    return pairs


def group_index():
    return (lax.axis_index("x") * 2 + lax.axis_index("zh")) * 2 + lax.axis_index("core")


def row_of(block):
    return ((block >> 4) << 3) + (block & 7)


def parity_of(block):
    return (block >> 3) & 1


def spread_adjoint(adj, left):
    wide = left.shape[1]
    entry = lax.broadcasted_iota(jnp.int32, (TILE, wide), 0)
    place = lax.broadcasted_iota(jnp.int32, (TILE, wide), 1)
    first = (entry >> 1) * 6
    spread = jnp.where((place >= first) & (place < first + 6), 1.0, 0.0).astype(jnp.bfloat16)
    column = lax.broadcasted_iota(jnp.int32, (32, TILE), 1)
    phase = lax.rem(lax.broadcasted_iota(jnp.int32, (32, wide), 1), 6)
    for b in range(2):
        for p in range(2):
            half = jnp.where((column & 1) == p, adj[b].astype(jnp.float32), 0.0)
            row = jnp.dot(
                half.astype(jnp.bfloat16), spread, preferred_element_type=jnp.float32
            )
            for q, (c, parity) in enumerate(LANE_PARTS):
                if parity == p:
                    at = (q * 2 + b) * 32
                    left[at : at + 32] = jnp.where(phase == 2 * c + b, row, 0.0).astype(
                        jnp.bfloat16
                    )


def terms_kernel(
    columns, lower, upper, adj, tiles, ours, own, side, mate, cross, on, sums, left, held, arrived
):
    copies = [
        pltpu.make_async_copy(tiles.at[k], held.at[k], arrived.at[k]) for k in range(17)
    ]
    for copy in copies:
        copy.start()
    odd, mine = lax.axis_index("core"), lax.axis_index("yp")
    quarter = mine * 2 + lax.axis_index("zp")
    off_base = GROUP_BLOCKS + HALO * odd
    on_base = GROUP_BLOCKS + HALO * (1 - odd)
    for i in range(ROWS):
        sums[i] = jnp.zeros(PLANES, jnp.float32)
    spread_adjoint(adj, left)
    low = lax.broadcasted_iota(jnp.int32, (32, 128), 1) < 64
    products = []
    for some in (range(9), range(9, 17)):
        for k in some:
            copies[k].wait()
        right = jnp.concatenate([held[k] for k in some], axis=1)
        every = jnp.dot(left[...], right, preferred_element_type=jnp.float32)
        products += [every[:, 128 * i : 128 * i + 128] for i in range(len(some))]
    for k in range(17):
        for b in range(2):
            t = [products[k][(q * 2 + b) * 32 : (q * 2 + b) * 32 + 32] for q in range(4)]
            main = t[0] + pltpu.roll(jnp.where(low, t[3], t[2]), 64, 1)
            tail = jnp.where(
                low[:16],
                t[1][:16] + pltpu.roll(t[3][:16], 64, 1),
                pltpu.roll(t[1][16:], 64, 1) + t[3][16:],
            )
            planes = jnp.concatenate([main, tail], axis=0)
            if k == 0:
                target = lax.axis_index("yh") * 8 + lax.axis_index("zq") * 4 + lax.axis_index("zp") * 2 + b
            else:
                c = columns[b, k - 1]
                slot = c - off_base
                target = jnp.where(
                    c < GROUP_BLOCKS,
                    ((parity_of(c) ^ mine) << 5) + row_of(c),
                    jnp.where(
                        (slot >= 0) & (slot < HALO),
                        OFF + (((slot >> 3) ^ quarter) << 3) + (slot & 7),
                        ON + c - on_base,
                    ),
                )
            sums[target] += planes
    ours[...] = sums[:OFF]
    own[...] = sums[OFF : OFF + 8]
    side[...] = sums[OFF + 8 : OFF + 16]
    mate[...] = sums[OFF + 16 : OFF + 24]
    cross[...] = sums[OFF + 24 : OFF + 32]
    on[...] = sums[ON : ON + HALO]


def quarter_kernel(side, mate, cross, own, leaving):
    leaving[...] = (own[...] + side[...]) + (mate[...] + cross[...])


def merge_kernel(lower, upper, got_on, ours, leaving, keep, give):
    sibling, odd = group_index() ^ 1, lax.axis_index("core")
    mine = lax.axis_index("yp")
    keep[...] = ours[KEEP : KEEP + 32]
    give[...] = ours[GIVE : GIVE + 32]
    for h in range(HALO):
        block = jnp.where(odd == 1, upper[sibling, h], lower[sibling, h])
        same = parity_of(block) == mine
        row = row_of(block)

        @pl.when(same)
        def _():
            keep[row] += got_on[h]

        @pl.when(jnp.logical_not(same))
        def _():
            give[row] += got_on[h]


def place_kernel(lower, upper, keep, got, crossed, passed, out):
    group, odd = group_index(), lax.axis_index("core")
    mine = lax.axis_index("yp")
    above = jnp.minimum(group + 1, lower.shape[0] - 1)
    below = jnp.maximum(group - 1, 0)
    out[...] = keep[...] + got[...]
    mirrored = 1 - lax.axis_index("zp")
    for i in range(8):
        for source, parity in ((crossed, mine), (passed, 1 - mine)):
            slot = parity * 16 + mirrored * 8 + i
            block = jnp.where(odd == 1, lower[above, slot], upper[below, slot])
            row = row_of(block)

            @pl.when(parity_of(block) == mine)
            def _():
                out[row] += source[i]


def spectral_kernel(matrix, adj, rates, out):
    for b in range(2):
        part = jnp.dot(
            matrix[...],
            adj[b].astype(jnp.float32),
            precision=lax.Precision.HIGHEST,
            preferred_element_type=jnp.float32,
        )
        out[b] = rates[b : b + 1, :] * part


def last_kernel(shared, part, precond, out):
    for b in range(2):
        total = shared[0, b]
        for i in range(1, 16):
            total += shared[i, b]
        tail = total[32:48]
        top = jnp.concatenate([total[:16], tail[:, :64]], axis=1)
        bottom = jnp.concatenate([total[16:32], tail[:, 64:]], axis=1)
        combined = (jnp.concatenate([top, bottom], axis=0) + part[b]).astype(jnp.bfloat16)
        out[b] = jnp.dot(combined, precond[b], preferred_element_type=jnp.float32).astype(
            jnp.bfloat16
        )


def whole():
    return pl.BlockSpec(memory_space=pltpu.VMEM)


def scalars():
    return pl.BlockSpec(memory_space=pltpu.SMEM)


def stack(*counts):
    return [jax.ShapeDtypeStruct((n,) + PLANES, jnp.float32) for n in counts]


def shards(adjoint, jacobian_tiles, columns, cell_rates, precond, lower_list, upper_list):
    blocks, row_count, tile_width = adjoint.shape
    slots = jacobian_tiles.shape[1]
    stored = slots, blocks * tile_width * tile_width // 128, 128
    tiles = jacobian_tiles.reshape(blocks, slots, -1, 128).transpose(1, 2, 0, 3).reshape(stored)
    square_precond = precond.reshape(blocks, tile_width, tile_width)
    padded = jnp.pad(
        adjoint.reshape(blocks, ADJ, INST, tile_width), ((0, 0), (0, 0), (0, 1), (0, 0))
    ).reshape(blocks, 32, tile_width)

    ours, own, side, mate, cross, on = pl.pallas_call(
        terms_kernel,
        out_shape=stack(OFF, 8, 8, 8, 8, HALO),
        in_specs=[scalars(), scalars(), scalars(), whole(), pl.BlockSpec(memory_space=pltpu.HBM)],
        out_specs=[whole()] * 6,
        scratch_shapes=[
            pltpu.VMEM((ROWS,) + PLANES, jnp.float32),
            pltpu.VMEM((256, stored[1]), jnp.bfloat16),
            pltpu.VMEM(stored, jnp.bfloat16),
            pltpu.SemaphoreType.DMA((slots,)),
        ],
        compiler_params=pltpu.CompilerParams(vmem_limit_bytes=50 * 2**20),
        name="terms",
    )(columns, lower_list, upper_list, padded, tiles)
    side = to_side(side)
    mate = to_mate(mate)
    cross = to_mates_side(cross)
    got_on = lax.ppermute(on, "core", [(0, 1), (1, 0)])
    leaving = pl.pallas_call(
        quarter_kernel,
        out_shape=stack(8)[0],
        in_specs=[whole()] * 4,
        out_specs=whole(),
        compiler_params=pltpu.CompilerParams(vmem_limit_bytes=16 * 2**20),
        name="quarter",
    )(side, mate, cross, own)
    crossed = lax.ppermute(leaving, ("x", "zh", "core", "zq", "zp"), off_chip_pairs())
    keep, give = pl.pallas_call(
        merge_kernel,
        out_shape=stack(32, 32),
        in_specs=[scalars(), scalars(), whole(), whole(), whole()],
        out_specs=[whole()] * 2,
        compiler_params=pltpu.CompilerParams(vmem_limit_bytes=24 * 2**20),
        name="merge",
    )(lower_list, upper_list, got_on, ours, leaving)
    got = to_mate(give)
    passed = to_mate(crossed)
    merged = pl.pallas_call(
        place_kernel,
        out_shape=stack(32)[0],
        in_specs=[scalars(), scalars()] + [whole()] * 4,
        out_specs=whole(),
        compiler_params=pltpu.CompilerParams(vmem_limit_bytes=16 * 2**20),
        name="place",
    )(lower_list, upper_list, keep, got, crossed, passed)
    shared = lax.all_to_all(merged.reshape(16, -1), ("yh", "zq", "zp"), 0, 0, tiled=True)

    half = jnp.pad(spectral_matrix(INST).T, ((0, 1), (0, 1)))
    matrix = jnp.kron(jnp.eye(ADJ, dtype=jnp.float32), half)
    part = pl.pallas_call(
        spectral_kernel,
        out_shape=jax.ShapeDtypeStruct((blocks, 32, tile_width), jnp.float32),
        in_specs=[whole()] * 3,
        out_specs=whole(),
        compiler_params=pltpu.CompilerParams(vmem_limit_bytes=8 * 2**20),
        name="spectral",
    )(matrix, padded, cell_rates)
    result = pl.pallas_call(
        last_kernel,
        out_shape=jax.ShapeDtypeStruct((blocks, 32, tile_width), jnp.bfloat16),
        in_specs=[whole()] * 3,
        out_specs=whole(),
        compiler_params=pltpu.CompilerParams(vmem_limit_bytes=8 * 2**20),
        name="last",
    )(shared.reshape(16, blocks, *PLANES), part, square_precond)
    return (
        result.reshape(blocks, ADJ, 16, tile_width)[:, :, :INST]
        .reshape(blocks, row_count, tile_width)
    )


def solution(mesh):
    split_mesh = Mesh(mesh.devices.reshape(SIZES), AXES)
    split = P(AXES)
    return jax.shard_map(
        shards,
        mesh=split_mesh,
        in_specs=(split, split, split, split, split, P(), P()),
        out_specs=split,
        check_vma=False,
    )
```

```python
import jax
import jax.numpy as jnp
from jax import lax
from jax.experimental import pallas as pl
from jax.experimental.pallas import tpu as pltpu
from jax.sharding import Mesh, PartitionSpec as P

INST = 15
ADJ = 2
HALO = 32
GROUP_BLOCKS = 64
AXES = ("x", "zh", "core", "yh", "yp", "zq", "zp")
SIZES = (4, 2, 2, 4, 2, 2, 2)
PLANES = (48, 128)
TILE = 192
LANE_PARTS = ((0, 0), (1, 0), (1, 1), (2, 1))
KEEP, GIVE, OFF, ON, ROWS = 0, 32, 64, 96, 128


def spectral_matrix(length):
    row_index = jnp.arange(length)[:, None]
    col_index = jnp.arange(length)[None, :]
    offset = row_index - col_index
    parity = jnp.where(offset % 2 == 0, 1.0, -1.0).astype(jnp.float32)
    phase_angle = jnp.pi / length * offset.astype(jnp.float32)
    sine_values = jnp.where(offset == 0, 1.0, jnp.sin(phase_angle))
    return jnp.where(offset == 0, 0.0, 0.5 * parity / sine_values)


def mate_of(core, y):
    return ((((y - core) % 8) ^ 1) + core) % 8


def to_mate(value):
    pairs = [(c * 8 + y, c * 8 + mate_of(c, y)) for c in range(2) for y in range(8)]
    return lax.ppermute(value, ("core", "yh", "yp"), pairs)


def to_side(value):
    return lax.ppermute(value, "zp", [(0, 1), (1, 0)])


def to_mates_side(value):
    pairs = [
        (c * 16 + y * 2 + z, c * 16 + mate_of(c, y) * 2 + 1 - z)
        for c in range(2)
        for y in range(8)
        for z in range(2)
    ]
    return lax.ppermute(value, ("core", "yh", "yp", "zp"), pairs)


def off_chip_pairs():
    pairs = []
    for g in range(16):
        t = g + 1 if g % 2 else g - 1
        if 0 <= t < 16:
            pairs += [(g * 4 + z, t * 4 + 3 - z) for z in range(4)]
    return pairs


def group_index():
    return (lax.axis_index("x") * 2 + lax.axis_index("zh")) * 2 + lax.axis_index("core")


def row_of(block):
    return ((block >> 4) << 3) + (block & 7)


def parity_of(block):
    return (block >> 3) & 1


def spread_adjoint(adj, left):
    wide = left.shape[1]
    entry = lax.broadcasted_iota(jnp.int32, (TILE, wide), 0)
    place = lax.broadcasted_iota(jnp.int32, (TILE, wide), 1)
    first = (entry >> 1) * 6
    spread = jnp.where((place >= first) & (place < first + 6), 1.0, 0.0).astype(jnp.bfloat16)
    column = lax.broadcasted_iota(jnp.int32, (32, TILE), 1)
    phase = lax.rem(lax.broadcasted_iota(jnp.int32, (32, wide), 1), 6)
    for b in range(2):
        for p in range(2):
            half = jnp.where((column & 1) == p, adj[b], 0.0)
            row = jnp.dot(
                half.astype(jnp.bfloat16), spread, preferred_element_type=jnp.float32
            )
            for q, (c, parity) in enumerate(LANE_PARTS):
                if parity == p:
                    at = (q * 2 + b) * 32
                    left[at : at + 32] = jnp.where(phase == 2 * c + b, row, 0.0).astype(
                        jnp.bfloat16
                    )


def terms_kernel(
    columns_in, adj_in, tiles,
    ours, own, side, mate, cross, on, rows,
    sums, left, held, adj, columns, arrived, loaded,
):
    small = (
        pltpu.make_async_copy(adj_in, adj, loaded.at[0]),
        pltpu.make_async_copy(columns_in, columns, loaded.at[1]),
    )
    copies = [
        pltpu.make_async_copy(tiles.at[k], held.at[k], arrived.at[k]) for k in range(17)
    ]
    for copy in small + tuple(copies):
        copy.start()
    odd, mine = lax.axis_index("core"), lax.axis_index("yp")
    quarter = mine * 2 + lax.axis_index("zp")
    off_base = GROUP_BLOCKS + HALO * odd
    on_base = GROUP_BLOCKS + HALO * (1 - odd)
    for i in range(ROWS):
        sums[i] = jnp.zeros(PLANES, jnp.float32)
    for copy in small:
        copy.wait()
    gap = jnp.zeros((1, TILE), jnp.float32)
    wide = adj[...].astype(jnp.float32)
    for b in range(2):
        row = wide[:, b, :]
        rows[b] = jnp.concatenate([row[:INST], gap, row[INST:], gap], axis=0)
    spread_adjoint(rows, left)
    low = lax.broadcasted_iota(jnp.int32, (32, 128), 1) < 64
    products = []
    for some in (range(9), range(9, 17)):
        for k in some:
            copies[k].wait()
        right = jnp.concatenate([held[k] for k in some], axis=1)
        every = jnp.dot(left[...], right, preferred_element_type=jnp.float32)
        products += [every[:, 128 * i : 128 * i + 128] for i in range(len(some))]
    for k in range(17):
        for b in range(2):
            t = [products[k][(q * 2 + b) * 32 : (q * 2 + b) * 32 + 32] for q in range(4)]
            main = t[0] + pltpu.roll(jnp.where(low, t[3], t[2]), 64, 1)
            tail = jnp.where(
                low[:16],
                t[1][:16] + pltpu.roll(t[3][:16], 64, 1),
                pltpu.roll(t[1][16:], 64, 1) + t[3][16:],
            )
            planes = jnp.concatenate([main, tail], axis=0)
            if k == 0:
                target = lax.axis_index("yh") * 8 + lax.axis_index("zq") * 4 + lax.axis_index("zp") * 2 + b
            else:
                c = columns[b, k - 1]
                slot = c - off_base
                target = jnp.where(
                    c < GROUP_BLOCKS,
                    ((parity_of(c) ^ mine) << 5) + row_of(c),
                    jnp.where(
                        (slot >= 0) & (slot < HALO),
                        OFF + (((slot >> 3) ^ quarter) << 3) + (slot & 7),
                        ON + c - on_base,
                    ),
                )
            sums[target] += planes
    ours[...] = sums[:OFF]
    own[...] = sums[OFF : OFF + 8]
    side[...] = sums[OFF + 8 : OFF + 16]
    mate[...] = sums[OFF + 16 : OFF + 24]
    cross[...] = sums[OFF + 24 : OFF + 32]
    on[...] = sums[ON : ON + HALO]


def quarter_kernel(side, mate, cross, own, leaving):
    leaving[...] = (own[...] + side[...]) + (mate[...] + cross[...])


def merge_kernel(lower, upper, got_on, ours, leaving, keep, give):
    sibling, odd = group_index() ^ 1, lax.axis_index("core")
    mine = lax.axis_index("yp")
    keep[...] = ours[KEEP : KEEP + 32]
    give[...] = ours[GIVE : GIVE + 32]
    for h in range(HALO):
        block = jnp.where(odd == 1, upper[sibling, h], lower[sibling, h])
        same = parity_of(block) == mine
        row = row_of(block)

        @pl.when(same)
        def _():
            keep[row] += got_on[h]

        @pl.when(jnp.logical_not(same))
        def _():
            give[row] += got_on[h]


def add_slots(lower, upper, source, parity, out):
    group, odd = group_index(), lax.axis_index("core")
    mine, mirrored = lax.axis_index("yp"), 1 - lax.axis_index("zp")
    above = jnp.minimum(group + 1, lower.shape[0] - 1)
    below = jnp.maximum(group - 1, 0)
    for i in range(8):
        slot = parity * 16 + mirrored * 8 + i
        block = jnp.where(odd == 1, lower[above, slot], upper[below, slot])
        row = row_of(block)

        @pl.when(parity_of(block) == mine)
        def _():
            out[row] += source[i]


def place_kernel(lower, upper, keep, got, crossed, out):
    out[...] = keep[...] + got[...]
    add_slots(lower, upper, crossed, lax.axis_index("yp"), out)


def finish_kernel(lower, upper, part, passed, out):
    out[...] = part[...]
    add_slots(lower, upper, passed, 1 - lax.axis_index("yp"), out)


def spectral_kernel(matrix, adj, rates, out):
    for b in range(2):
        part = jnp.dot(
            matrix[...],
            adj[b],
            precision=lax.Precision.HIGHEST,
            preferred_element_type=jnp.float32,
        )
        out[b] = rates[b : b + 1, :] * part


def last_kernel(shared, part, precond, out):
    for b in range(2):
        total = shared[0, b]
        for i in range(1, 16):
            total += shared[i, b]
        tail = total[32:48]
        top = jnp.concatenate([total[:16], tail[:, :64]], axis=1)
        bottom = jnp.concatenate([total[16:32], tail[:, 64:]], axis=1)
        combined = (jnp.concatenate([top, bottom], axis=0) + part[b]).astype(jnp.bfloat16)
        out[b] = jnp.dot(combined, precond[b], preferred_element_type=jnp.float32).astype(
            jnp.bfloat16
        )


def whole():
    return pl.BlockSpec(memory_space=pltpu.VMEM)


def scalars():
    return pl.BlockSpec(memory_space=pltpu.SMEM)


def in_hbm(*arrays):
    return [pltpu.with_memory_space_constraint(a, pltpu.HBM) for a in arrays]


def stack(*counts):
    return [jax.ShapeDtypeStruct((n,) + PLANES, jnp.float32) for n in counts]


def shards(adjoint, jacobian_tiles, columns, cell_rates, precond, lower_list, upper_list):
    blocks, row_count, tile_width = adjoint.shape
    slots = jacobian_tiles.shape[1]
    stored = slots, blocks * tile_width * tile_width // 128, 128
    tiles = jacobian_tiles.reshape(blocks, slots, -1, 128).transpose(1, 2, 0, 3).reshape(stored)
    square_precond = precond.reshape(blocks, tile_width, tile_width)

    ours, own, side, mate, cross, on, rows = pl.pallas_call(
        terms_kernel,
        out_shape=stack(OFF, 8, 8, 8, 8, HALO)
        + [jax.ShapeDtypeStruct((blocks, 32, tile_width), jnp.float32)],
        in_specs=[pl.BlockSpec(memory_space=pltpu.HBM)] * 3,
        out_specs=[whole()] * 7,
        scratch_shapes=[
            pltpu.VMEM((ROWS,) + PLANES, jnp.float32),
            pltpu.VMEM((256, stored[1]), jnp.bfloat16),
            pltpu.VMEM(stored, jnp.bfloat16),
            pltpu.VMEM((row_count, blocks, tile_width), jnp.bfloat16),
            pltpu.SMEM(columns.shape, jnp.int32),
            pltpu.SemaphoreType.DMA((slots,)),
            pltpu.SemaphoreType.DMA((2,)),
        ],
        compiler_params=pltpu.CompilerParams(vmem_limit_bytes=50 * 2**20),
        name="terms",
    )(*in_hbm(columns, adjoint.transpose(1, 0, 2), tiles))
    side = to_side(side)
    mate = to_mate(mate)
    cross = to_mates_side(cross)
    got_on = lax.ppermute(on, "core", [(0, 1), (1, 0)])
    leaving = pl.pallas_call(
        quarter_kernel,
        out_shape=stack(8)[0],
        in_specs=[whole()] * 4,
        out_specs=whole(),
        compiler_params=pltpu.CompilerParams(vmem_limit_bytes=16 * 2**20),
        name="quarter",
    )(side, mate, cross, own)
    crossed = lax.ppermute(leaving, ("x", "zh", "core", "zq", "zp"), off_chip_pairs())
    keep, give = pl.pallas_call(
        merge_kernel,
        out_shape=stack(32, 32),
        in_specs=[scalars(), scalars(), whole(), whole(), whole()],
        out_specs=[whole()] * 2,
        compiler_params=pltpu.CompilerParams(vmem_limit_bytes=24 * 2**20),
        name="merge",
    )(lower_list, upper_list, got_on, ours, leaving)
    got = to_mate(give)
    passed = to_mate(crossed)
    merged = keep
    for kernel, arrays in ((place_kernel, (got, crossed)), (finish_kernel, (passed,))):
        merged = pl.pallas_call(
            kernel,
            out_shape=stack(32)[0],
            in_specs=[scalars(), scalars()] + [whole()] * (1 + len(arrays)),
            out_specs=whole(),
            compiler_params=pltpu.CompilerParams(vmem_limit_bytes=16 * 2**20),
            cost_estimate=pl.CostEstimate(flops=2**20, bytes_accessed=2**22, transcendentals=0),
        )(lower_list, upper_list, merged, *arrays)
    shared = lax.all_to_all(merged.reshape(16, -1), ("yh", "zq", "zp"), 0, 0, tiled=True)

    half = jnp.pad(spectral_matrix(INST).T, ((0, 1), (0, 1)))
    matrix = jnp.kron(jnp.eye(ADJ, dtype=jnp.float32), half)
    part = pl.pallas_call(
        spectral_kernel,
        out_shape=jax.ShapeDtypeStruct((blocks, 32, tile_width), jnp.float32),
        in_specs=[whole()] * 3,
        out_specs=whole(),
        compiler_params=pltpu.CompilerParams(vmem_limit_bytes=8 * 2**20),
        name="spectral",
    )(matrix, rows, cell_rates)
    result = pl.pallas_call(
        last_kernel,
        out_shape=jax.ShapeDtypeStruct((blocks, 32, tile_width), jnp.bfloat16),
        in_specs=[whole()] * 3,
        out_specs=whole(),
        compiler_params=pltpu.CompilerParams(vmem_limit_bytes=8 * 2**20),
        name="last",
    )(shared.reshape(16, blocks, *PLANES), part, square_precond)
    return (
        result.reshape(blocks, ADJ, 16, tile_width)[:, :, :INST]
        .reshape(blocks, row_count, tile_width)
    )


def solution(mesh):
    split_mesh = Mesh(mesh.devices.reshape(SIZES), AXES)
    split = P(AXES)
    return jax.shard_map(
        shards,
        mesh=split_mesh,
        in_specs=(split, split, split, split, split, P(), P()),
        out_specs=split,
        check_vma=False,
    )
```

```python
import jax
import jax.numpy as jnp
from jax import lax
from jax.experimental import pallas as pl
from jax.experimental.pallas import tpu as pltpu
from jax.sharding import Mesh, PartitionSpec as P

INST = 15
ADJ = 2
HALO = 32
GROUP_BLOCKS = 64
AXES = ("x", "zh", "core", "yh", "yp", "zq", "zp")
SIZES = (4, 2, 2, 4, 2, 2, 2)
PLANES = (48, 128)
TILE = 192
LANE_PARTS = ((0, 0), (1, 0), (1, 1), (2, 1))
KEEP, GIVE, OFF, ON, ROWS = 0, 32, 64, 96, 128


def spectral_matrix(length):
    row_index = jnp.arange(length)[:, None]
    col_index = jnp.arange(length)[None, :]
    offset = row_index - col_index
    parity = jnp.where(offset % 2 == 0, 1.0, -1.0).astype(jnp.float32)
    phase_angle = jnp.pi / length * offset.astype(jnp.float32)
    sine_values = jnp.where(offset == 0, 1.0, jnp.sin(phase_angle))
    return jnp.where(offset == 0, 0.0, 0.5 * parity / sine_values)


def mate_of(core, y):
    return ((((y - core) % 8) ^ 1) + core) % 8


def to_mate(value):
    pairs = [(c * 8 + y, c * 8 + mate_of(c, y)) for c in range(2) for y in range(8)]
    return lax.ppermute(value, ("core", "yh", "yp"), pairs)


def to_side(value):
    return lax.ppermute(value, "zp", [(0, 1), (1, 0)])


def to_mates_side(value):
    pairs = [
        (c * 16 + y * 2 + z, c * 16 + mate_of(c, y) * 2 + 1 - z)
        for c in range(2)
        for y in range(8)
        for z in range(2)
    ]
    return lax.ppermute(value, ("core", "yh", "yp", "zp"), pairs)


def off_chip_pairs():
    pairs = []
    for g in range(16):
        t = g + 1 if g % 2 else g - 1
        if 0 <= t < 16:
            pairs += [(g * 4 + z, t * 4 + 3 - z) for z in range(4)]
    return pairs


def group_index():
    return (lax.axis_index("x") * 2 + lax.axis_index("zh")) * 2 + lax.axis_index("core")


def row_of(block):
    return (((block >> 1) & 3) << 3) + ((block >> 4) << 1) + (block & 1)


def parity_of(block):
    return (block >> 3) & 1


def spread_adjoint(adj, left):
    wide = left.shape[1]
    entry = lax.broadcasted_iota(jnp.int32, (TILE, wide), 0)
    place = lax.broadcasted_iota(jnp.int32, (TILE, wide), 1)
    first = (entry >> 1) * 6
    spread = jnp.where((place >= first) & (place < first + 6), 1.0, 0.0).astype(jnp.bfloat16)
    column = lax.broadcasted_iota(jnp.int32, (32, TILE), 1)
    phase = lax.rem(lax.broadcasted_iota(jnp.int32, (32, wide), 1), 6)
    for b in range(2):
        for p in range(2):
            half = jnp.where((column & 1) == p, adj[b], 0.0)
            row = jnp.dot(
                half.astype(jnp.bfloat16), spread, preferred_element_type=jnp.float32
            )
            for q, (c, parity) in enumerate(LANE_PARTS):
                if parity == p:
                    at = (q * 2 + b) * 32
                    left[at : at + 32] = jnp.where(phase == 2 * c + b, row, 0.0).astype(
                        jnp.bfloat16
                    )


def terms_kernel(
    columns_in, adj_in, tiles,
    ours, own, side, mate, cross, on, rows,
    sums, left, held, adj, columns, arrived, loaded,
):
    small = (
        pltpu.make_async_copy(adj_in, adj, loaded.at[0]),
        pltpu.make_async_copy(columns_in, columns, loaded.at[1]),
    )
    copies = [
        pltpu.make_async_copy(tiles.at[k], held.at[k], arrived.at[k]) for k in range(17)
    ]
    for copy in small + tuple(copies):
        copy.start()
    odd, mine = lax.axis_index("core"), lax.axis_index("yp")
    quarter = mine * 2 + lax.axis_index("zp")
    off_base = GROUP_BLOCKS + HALO * odd
    on_base = GROUP_BLOCKS + HALO * (1 - odd)
    for i in range(ROWS):
        sums[i] = jnp.zeros(PLANES, jnp.float32)
    for copy in small:
        copy.wait()
    gap = jnp.zeros((1, TILE), jnp.float32)
    wide = adj[...].astype(jnp.float32)
    for b in range(2):
        row = wide[:, b, :]
        rows[b] = jnp.concatenate([row[:INST], gap, row[INST:], gap], axis=0)
    spread_adjoint(rows, left)
    low = lax.broadcasted_iota(jnp.int32, (32, 128), 1) < 64
    products = []
    for some in (range(9), range(9, 17)):
        for k in some:
            copies[k].wait()
        right = jnp.concatenate([held[k] for k in some], axis=1)
        every = jnp.dot(left[...], right, preferred_element_type=jnp.float32)
        products += [every[:, 128 * i : 128 * i + 128] for i in range(len(some))]
    for k in range(17):
        for b in range(2):
            t = [products[k][(q * 2 + b) * 32 : (q * 2 + b) * 32 + 32] for q in range(4)]
            main = t[0] + pltpu.roll(jnp.where(low, t[3], t[2]), 64, 1)
            tail = jnp.where(
                low[:16],
                t[1][:16] + pltpu.roll(t[3][:16], 64, 1),
                pltpu.roll(t[1][16:], 64, 1) + t[3][16:],
            )
            planes = jnp.concatenate([main, tail], axis=0)
            if k == 0:
                target = lax.axis_index("zq") * 16 + lax.axis_index("zp") * 8 + lax.axis_index("yh") * 2 + b
            else:
                c = columns[b, k - 1]
                slot = c - off_base
                target = jnp.where(
                    c < GROUP_BLOCKS,
                    ((parity_of(c) ^ mine) << 5) + row_of(c),
                    jnp.where(
                        (slot >= 0) & (slot < HALO),
                        OFF + (((slot >> 3) ^ quarter) << 3) + (slot & 7),
                        ON + c - on_base,
                    ),
                )
            sums[target] += planes
    ours[...] = sums[:OFF]
    own[...] = sums[OFF : OFF + 8]
    side[...] = sums[OFF + 8 : OFF + 16]
    mate[...] = sums[OFF + 16 : OFF + 24]
    cross[...] = sums[OFF + 24 : OFF + 32]
    on[...] = sums[ON : ON + HALO]


def quarter_kernel(side, mate, cross, own, leaving):
    leaving[...] = (own[...] + side[...]) + (mate[...] + cross[...])


def merge_kernel(lower, upper, got_on, ours, leaving, keep, give):
    sibling, odd = group_index() ^ 1, lax.axis_index("core")
    mine = lax.axis_index("yp")
    keep[...] = ours[KEEP : KEEP + 32]
    give[...] = ours[GIVE : GIVE + 32]
    for h in range(HALO):
        block = jnp.where(odd == 1, upper[sibling, h], lower[sibling, h])
        same = parity_of(block) == mine
        row = row_of(block)

        @pl.when(same)
        def _():
            keep[row] += got_on[h]

        @pl.when(jnp.logical_not(same))
        def _():
            give[row] += got_on[h]


def add_slots(lower, upper, source, parity, out):
    group, odd = group_index(), lax.axis_index("core")
    mine, mirrored = lax.axis_index("yp"), 1 - lax.axis_index("zp")
    above = jnp.minimum(group + 1, lower.shape[0] - 1)
    below = jnp.maximum(group - 1, 0)
    for i in range(8):
        slot = parity * 16 + mirrored * 8 + i
        block = jnp.where(odd == 1, lower[above, slot], upper[below, slot])
        row = row_of(block)

        @pl.when(parity_of(block) == mine)
        def _():
            out[row] += source[i]


def place_kernel(lower, upper, keep, crossed, out):
    out[...] = keep[...]
    add_slots(lower, upper, crossed, lax.axis_index("yp"), out)


def finish_kernel(lower, upper, part, got, passed, out):
    out[...] = part[...] + got[...]
    add_slots(lower, upper, passed, 1 - lax.axis_index("yp"), out)


def spectral_kernel(matrix, adj, rates, out):
    for b in range(2):
        part = jnp.dot(
            matrix[...],
            adj[b],
            precision=lax.Precision.HIGHEST,
            preferred_element_type=jnp.float32,
        )
        out[b] = rates[b : b + 1, :] * part


def last_kernel(shared, part, precond, out):
    results = []
    for b in range(2):
        total = shared[0, b]
        for i in range(1, 16):
            total += shared[i, b]
        tail = total[32:48]
        top = jnp.concatenate([total[:16], tail[:, :64]], axis=1)
        bottom = jnp.concatenate([total[16:32], tail[:, 64:]], axis=1)
        combined = (jnp.concatenate([top, bottom], axis=0) + part[b]).astype(jnp.bfloat16)
        result = jnp.dot(combined, precond[b], preferred_element_type=jnp.float32)
        results.append(jnp.concatenate([result[:INST], result[16 : 16 + INST]], axis=0))
    out[...] = jnp.stack(results, axis=1).astype(jnp.bfloat16)


def whole():
    return pl.BlockSpec(memory_space=pltpu.VMEM)


def scalars():
    return pl.BlockSpec(memory_space=pltpu.SMEM)


def in_hbm(*arrays):
    return [pltpu.with_memory_space_constraint(a, pltpu.HBM) for a in arrays]


def stack(*counts):
    return [jax.ShapeDtypeStruct((n,) + PLANES, jnp.float32) for n in counts]


def shards(adjoint, jacobian_tiles, columns, cell_rates, precond, lower_list, upper_list):
    blocks, row_count, tile_width = adjoint.shape
    slots = jacobian_tiles.shape[1]
    stored = slots, blocks * tile_width * tile_width // 128, 128
    tiles = jacobian_tiles.reshape(blocks, slots, -1, 128).transpose(1, 2, 0, 3).reshape(stored)
    square_precond = precond.reshape(blocks, tile_width, tile_width)

    ours, own, side, mate, cross, on, rows = pl.pallas_call(
        terms_kernel,
        out_shape=stack(OFF, 8, 8, 8, 8, HALO)
        + [jax.ShapeDtypeStruct((blocks, 32, tile_width), jnp.float32)],
        in_specs=[pl.BlockSpec(memory_space=pltpu.HBM)] * 3,
        out_specs=[whole()] * 7,
        scratch_shapes=[
            pltpu.VMEM((ROWS,) + PLANES, jnp.float32),
            pltpu.VMEM((256, stored[1]), jnp.bfloat16),
            pltpu.VMEM(stored, jnp.bfloat16),
            pltpu.VMEM((row_count, blocks, tile_width), jnp.bfloat16),
            pltpu.SMEM(columns.shape, jnp.int32),
            pltpu.SemaphoreType.DMA((slots,)),
            pltpu.SemaphoreType.DMA((2,)),
        ],
        compiler_params=pltpu.CompilerParams(vmem_limit_bytes=50 * 2**20),
        name="terms",
    )(*in_hbm(columns, adjoint.transpose(1, 0, 2), tiles))
    side = to_side(side)
    mate = to_mate(mate)
    cross = to_mates_side(cross)
    got_on = lax.ppermute(on, "core", [(0, 1), (1, 0)])
    leaving = pl.pallas_call(
        quarter_kernel,
        out_shape=stack(8)[0],
        in_specs=[whole()] * 4,
        out_specs=whole(),
        compiler_params=pltpu.CompilerParams(vmem_limit_bytes=16 * 2**20),
        name="quarter",
    )(side, mate, cross, own)
    crossed = lax.ppermute(leaving, ("x", "zh", "core", "zq", "zp"), off_chip_pairs())
    keep, give = pl.pallas_call(
        merge_kernel,
        out_shape=stack(32, 32),
        in_specs=[scalars(), scalars(), whole(), whole(), whole()],
        out_specs=[whole()] * 2,
        compiler_params=pltpu.CompilerParams(vmem_limit_bytes=24 * 2**20),
        name="merge",
    )(lower_list, upper_list, got_on, ours, leaving)
    got = to_mate(give)
    passed = to_mate(crossed)
    merged = keep
    for kernel, arrays in ((place_kernel, (crossed,)), (finish_kernel, (got, passed))):
        merged = pl.pallas_call(
            kernel,
            out_shape=stack(32)[0],
            in_specs=[scalars(), scalars()] + [whole()] * (1 + len(arrays)),
            out_specs=whole(),
            compiler_params=pltpu.CompilerParams(vmem_limit_bytes=16 * 2**20),
            cost_estimate=pl.CostEstimate(flops=2**20, bytes_accessed=2**22, transcendentals=0),
        )(lower_list, upper_list, merged, *arrays)
    shared = lax.all_to_all(merged.reshape(16, -1), ("zq", "zp", "yh"), 0, 0, tiled=True)

    half = jnp.pad(spectral_matrix(INST).T, ((0, 1), (0, 1)))
    matrix = jnp.kron(jnp.eye(ADJ, dtype=jnp.float32), half)
    part = pl.pallas_call(
        spectral_kernel,
        out_shape=jax.ShapeDtypeStruct((blocks, 32, tile_width), jnp.float32),
        in_specs=[whole()] * 3,
        out_specs=whole(),
        compiler_params=pltpu.CompilerParams(vmem_limit_bytes=8 * 2**20),
        name="spectral",
    )(matrix, rows, cell_rates)
    result = pl.pallas_call(
        last_kernel,
        out_shape=jax.ShapeDtypeStruct((row_count, blocks, tile_width), jnp.bfloat16),
        in_specs=[whole()] * 3,
        out_specs=whole(),
        compiler_params=pltpu.CompilerParams(vmem_limit_bytes=8 * 2**20),
        name="last",
    )(shared.reshape(16, blocks, *PLANES), part, square_precond)
    return result.transpose(1, 0, 2)


def solution(mesh):
    split_mesh = Mesh(mesh.devices.reshape(SIZES), AXES)
    split = P(AXES)
    return jax.shard_map(
        shards,
        mesh=split_mesh,
        in_specs=(split, split, split, split, split, P(), P()),
        out_specs=split,
        check_vma=False,
    )
```

```python
import jax
import jax.numpy as jnp
from jax import lax
from jax.experimental import pallas as pl
from jax.experimental.pallas import tpu as pltpu
from jax.sharding import Mesh, PartitionSpec as P

INST = 15
ADJ = 2
HALO = 32
GROUP_BLOCKS = 64
AXES = ("x", "zh", "core", "yh", "yp", "zq", "zp")
SIZES = (4, 2, 2, 4, 2, 2, 2)
PLANES = (48, 128)
TILE = 192
LANE_PARTS = ((0, 0), (1, 0), (1, 1), (2, 1))
KEEP, GIVE, OFF, ON, ROWS = 0, 32, 64, 96, 128


def spectral_matrix(length):
    row_index = jnp.arange(length)[:, None]
    col_index = jnp.arange(length)[None, :]
    offset = row_index - col_index
    parity = jnp.where(offset % 2 == 0, 1.0, -1.0).astype(jnp.float32)
    phase_angle = jnp.pi / length * offset.astype(jnp.float32)
    sine_values = jnp.where(offset == 0, 1.0, jnp.sin(phase_angle))
    return jnp.where(offset == 0, 0.0, 0.5 * parity / sine_values)


def mate_of(core, y):
    return ((((y - core) % 8) ^ 1) + core) % 8


def to_mate(value):
    pairs = [(c * 8 + y, c * 8 + mate_of(c, y)) for c in range(2) for y in range(8)]
    return lax.ppermute(value, ("core", "yh", "yp"), pairs)


def to_side(value):
    return lax.ppermute(value, "zp", [(0, 1), (1, 0)])


def to_mates_side(value):
    pairs = [
        (c * 16 + y * 2 + z, c * 16 + mate_of(c, y) * 2 + 1 - z)
        for c in range(2)
        for y in range(8)
        for z in range(2)
    ]
    return lax.ppermute(value, ("core", "yh", "yp", "zp"), pairs)


def off_chip_pairs():
    pairs = []
    for g in range(16):
        t = g + 1 if g % 2 else g - 1
        if 0 <= t < 16:
            pairs += [(g * 4 + z, t * 4 + 3 - z) for z in range(4)]
    return pairs


def group_index():
    return (lax.axis_index("x") * 2 + lax.axis_index("zh")) * 2 + lax.axis_index("core")


def row_of(block):
    return ((block >> 4) << 3) + (block & 7)


def parity_of(block):
    return (block >> 3) & 1


def spread_adjoint(adj, left):
    wide = left.shape[1]
    entry = lax.broadcasted_iota(jnp.int32, (TILE, wide), 0)
    place = lax.broadcasted_iota(jnp.int32, (TILE, wide), 1)
    first = (entry >> 1) * 6
    spread = jnp.where((place >= first) & (place < first + 6), 1.0, 0.0).astype(jnp.bfloat16)
    column = lax.broadcasted_iota(jnp.int32, (32, TILE), 1)
    phase = lax.rem(lax.broadcasted_iota(jnp.int32, (32, wide), 1), 6)
    for b in range(2):
        for p in range(2):
            half = jnp.where((column & 1) == p, adj[b], 0.0)
            row = jnp.dot(
                half.astype(jnp.bfloat16), spread, preferred_element_type=jnp.float32
            )
            for q, (c, parity) in enumerate(LANE_PARTS):
                if parity == p:
                    at = (q * 2 + b) * 32
                    left[at : at + 32] = jnp.where(phase == 2 * c + b, row, 0.0).astype(
                        jnp.bfloat16
                    )


def terms_kernel(
    columns_in, adj_in, tiles,
    ours, own, side, mate, cross, on, rows,
    sums, left, held, adj, columns, arrived, loaded,
):
    small = (
        pltpu.make_async_copy(adj_in, adj, loaded.at[0]),
        pltpu.make_async_copy(columns_in, columns, loaded.at[1]),
    )
    copies = [
        pltpu.make_async_copy(tiles.at[k], held.at[k], arrived.at[k]) for k in range(17)
    ]
    for copy in small + tuple(copies):
        copy.start()
    odd, mine = lax.axis_index("core"), lax.axis_index("yp")
    quarter = mine * 2 + lax.axis_index("zp")
    off_base = GROUP_BLOCKS + HALO * odd
    on_base = GROUP_BLOCKS + HALO * (1 - odd)
    for i in range(ROWS):
        sums[i] = jnp.zeros(PLANES, jnp.float32)
    for copy in small:
        copy.wait()
    gap = jnp.zeros((1, TILE), jnp.float32)
    wide = adj[...].astype(jnp.float32)
    for b in range(2):
        row = wide[:, b, :]
        rows[b] = jnp.concatenate([row[:INST], gap, row[INST:], gap], axis=0)
    spread_adjoint(rows, left)
    low = lax.broadcasted_iota(jnp.int32, (32, 128), 1) < 64
    products = []
    for some in (range(9), range(9, 17)):
        for k in some:
            copies[k].wait()
        right = jnp.concatenate([held[k] for k in some], axis=1)
        every = jnp.dot(left[...], right, preferred_element_type=jnp.float32)
        products += [every[:, 128 * i : 128 * i + 128] for i in range(len(some))]
    for k in range(17):
        for b in range(2):
            t = [products[k][(q * 2 + b) * 32 : (q * 2 + b) * 32 + 32] for q in range(4)]
            main = t[0] + pltpu.roll(jnp.where(low, t[3], t[2]), 64, 1)
            tail = jnp.where(
                low[:16],
                t[1][:16] + pltpu.roll(t[3][:16], 64, 1),
                pltpu.roll(t[1][16:], 64, 1) + t[3][16:],
            )
            planes = jnp.concatenate([main, tail], axis=0)
            if k == 0:
                target = lax.axis_index("yh") * 8 + lax.axis_index("zq") * 4 + lax.axis_index("zp") * 2 + b
            else:
                c = columns[b, k - 1]
                slot = c - off_base
                target = jnp.where(
                    c < GROUP_BLOCKS,
                    ((parity_of(c) ^ mine) << 5) + row_of(c),
                    jnp.where(
                        (slot >= 0) & (slot < HALO),
                        OFF + (((slot >> 3) ^ quarter) << 3) + (slot & 7),
                        ON + c - on_base,
                    ),
                )
            sums[target] += planes
    ours[...] = sums[:OFF]
    own[...] = sums[OFF : OFF + 8]
    side[...] = sums[OFF + 8 : OFF + 16]
    mate[...] = sums[OFF + 16 : OFF + 24]
    cross[...] = sums[OFF + 24 : OFF + 32]
    on[...] = sums[ON : ON + HALO]


def quarter_kernel(side, mate, cross, own, leaving):
    leaving[...] = (own[...] + side[...]) + (mate[...] + cross[...])


def merge_kernel(lower, upper, got_on, ours, leaving, keep, give):
    sibling, odd = group_index() ^ 1, lax.axis_index("core")
    mine = lax.axis_index("yp")
    keep[...] = ours[KEEP : KEEP + 32]
    give[...] = ours[GIVE : GIVE + 32]
    for h in range(HALO):
        block = jnp.where(odd == 1, upper[sibling, h], lower[sibling, h])
        same = parity_of(block) == mine
        row = row_of(block)

        @pl.when(same)
        def _():
            keep[row] += got_on[h]

        @pl.when(jnp.logical_not(same))
        def _():
            give[row] += got_on[h]


def add_slots(lower, upper, source, parity, out):
    group, odd = group_index(), lax.axis_index("core")
    mine, mirrored = lax.axis_index("yp"), 1 - lax.axis_index("zp")
    above = jnp.minimum(group + 1, lower.shape[0] - 1)
    below = jnp.maximum(group - 1, 0)
    for i in range(8):
        slot = parity * 16 + mirrored * 8 + i
        block = jnp.where(odd == 1, lower[above, slot], upper[below, slot])
        row = row_of(block)

        @pl.when(parity_of(block) == mine)
        def _():
            out[row] += source[i]


def place_kernel(lower, upper, keep, crossed, out):
    out[...] = keep[...]
    add_slots(lower, upper, crossed, lax.axis_index("yp"), out)


def finish_kernel(lower, upper, part, got, passed, out):
    out[...] = part[...] + got[...]
    add_slots(lower, upper, passed, 1 - lax.axis_index("yp"), out)


def spectral_kernel(matrix, adj, rates, out):
    for b in range(2):
        part = jnp.dot(
            matrix[...],
            adj[b],
            precision=lax.Precision.HIGHEST,
            preferred_element_type=jnp.float32,
        )
        out[b] = rates[b : b + 1, :] * part


def last_kernel(shared, part, precond, out):
    results = []
    for b in range(2):
        total = shared[0, b]
        for i in range(1, 16):
            total += shared[i, b]
        tail = total[32:48]
        top = jnp.concatenate([total[:16], tail[:, :64]], axis=1)
        bottom = jnp.concatenate([total[16:32], tail[:, 64:]], axis=1)
        combined = (jnp.concatenate([top, bottom], axis=0) + part[b]).astype(jnp.bfloat16)
        result = jnp.dot(combined, precond[b], preferred_element_type=jnp.float32)
        results.append(jnp.concatenate([result[:INST], result[16 : 16 + INST]], axis=0))
    out[...] = jnp.stack(results, axis=1).astype(jnp.bfloat16)


def whole():
    return pl.BlockSpec(memory_space=pltpu.VMEM)


def scalars():
    return pl.BlockSpec(memory_space=pltpu.SMEM)


def in_hbm(*arrays):
    return [pltpu.with_memory_space_constraint(a, pltpu.HBM) for a in arrays]


def stack(*counts):
    return [jax.ShapeDtypeStruct((n,) + PLANES, jnp.float32) for n in counts]


def shards(adjoint, jacobian_tiles, columns, cell_rates, precond, lower_list, upper_list):
    blocks, row_count, tile_width = adjoint.shape
    slots = jacobian_tiles.shape[1]
    stored = slots, blocks * tile_width * tile_width // 128, 128
    tiles = jacobian_tiles.reshape(blocks, slots, -1, 128).transpose(1, 2, 0, 3).reshape(stored)
    square_precond = precond.reshape(blocks, tile_width, tile_width)

    ours, own, side, mate, cross, on, rows = pl.pallas_call(
        terms_kernel,
        out_shape=stack(OFF, 8, 8, 8, 8, HALO)
        + [jax.ShapeDtypeStruct((blocks, 32, tile_width), jnp.float32)],
        in_specs=[pl.BlockSpec(memory_space=pltpu.HBM)] * 3,
        out_specs=[whole()] * 7,
        scratch_shapes=[
            pltpu.VMEM((ROWS,) + PLANES, jnp.float32),
            pltpu.VMEM((256, stored[1]), jnp.bfloat16),
            pltpu.VMEM(stored, jnp.bfloat16),
            pltpu.VMEM((row_count, blocks, tile_width), jnp.bfloat16),
            pltpu.SMEM(columns.shape, jnp.int32),
            pltpu.SemaphoreType.DMA((slots,)),
            pltpu.SemaphoreType.DMA((2,)),
        ],
        compiler_params=pltpu.CompilerParams(vmem_limit_bytes=50 * 2**20),
        name="terms",
    )(*in_hbm(columns, adjoint.transpose(1, 0, 2), tiles))
    side = to_side(side)
    mate = to_mate(mate)
    cross = to_mates_side(cross)
    got_on = lax.ppermute(on, "core", [(0, 1), (1, 0)])
    leaving = pl.pallas_call(
        quarter_kernel,
        out_shape=stack(8)[0],
        in_specs=[whole()] * 4,
        out_specs=whole(),
        compiler_params=pltpu.CompilerParams(vmem_limit_bytes=16 * 2**20),
        name="quarter",
    )(side, mate, cross, own)
    crossed = lax.ppermute(leaving, ("x", "zh", "core", "zq", "zp"), off_chip_pairs())
    keep, give = pl.pallas_call(
        merge_kernel,
        out_shape=stack(32, 32),
        in_specs=[scalars(), scalars(), whole(), whole(), whole()],
        out_specs=[whole()] * 2,
        compiler_params=pltpu.CompilerParams(vmem_limit_bytes=24 * 2**20),
        name="merge",
    )(lower_list, upper_list, got_on, ours, leaving)
    got = to_mate(give)
    passed = to_mate(crossed)
    merged = keep
    for kernel, arrays in ((place_kernel, (crossed,)), (finish_kernel, (got, passed))):
        merged = pl.pallas_call(
            kernel,
            out_shape=stack(32)[0],
            in_specs=[scalars(), scalars()] + [whole()] * (1 + len(arrays)),
            out_specs=whole(),
            compiler_params=pltpu.CompilerParams(vmem_limit_bytes=16 * 2**20),
            cost_estimate=pl.CostEstimate(flops=2**20, bytes_accessed=2**22, transcendentals=0),
        )(lower_list, upper_list, merged, *arrays)
    shared = lax.all_to_all(merged.reshape(16, -1), ("yh", "zq", "zp"), 0, 0, tiled=True)

    half = jnp.pad(spectral_matrix(INST).T, ((0, 1), (0, 1)))
    matrix = jnp.kron(jnp.eye(ADJ, dtype=jnp.float32), half)
    part = pl.pallas_call(
        spectral_kernel,
        out_shape=jax.ShapeDtypeStruct((blocks, 32, tile_width), jnp.float32),
        in_specs=[whole()] * 3,
        out_specs=whole(),
        compiler_params=pltpu.CompilerParams(vmem_limit_bytes=8 * 2**20),
        name="spectral",
    )(matrix, rows, cell_rates)
    result = pl.pallas_call(
        last_kernel,
        out_shape=jax.ShapeDtypeStruct((row_count, blocks, tile_width), jnp.bfloat16),
        in_specs=[whole()] * 3,
        out_specs=whole(),
        compiler_params=pltpu.CompilerParams(vmem_limit_bytes=8 * 2**20),
        name="last",
    )(shared.reshape(16, blocks, *PLANES), part, square_precond)
    return result.transpose(1, 0, 2)


def solution(mesh):
    split_mesh = Mesh(mesh.devices.reshape(SIZES), AXES)
    split = P(AXES)
    return jax.shard_map(
        shards,
        mesh=split_mesh,
        in_specs=(split, split, split, split, split, P(), P()),
        out_specs=split,
        check_vma=False,
    )
```
